512 devices in a mesh: tile: 16 (over x, y_hi, core), pos: 32 (over z, y_lo).
Axes of the slice: x: 4, y: 4 (y_hi: 2, y_lo: 2; y = y_hi * 2 + y_lo), z: 16, core: 2. Of those that a mesh axis runs over, the one named last changes fastest.
Arguments:
- patterns: bfloat16 [8192, 128, 128], P(('tile', 'pos')), may hold values from 0 to 2
- coords: int32 [8192, 2], P(('tile', 'pos')), may hold values from 0 to 2047, as said below
- send_slots: int32 [512, 16, 2], P(('tile', 'pos')), may hold values from 0 to 15, as said below
- send_counts: int32 [512, 16], P(('tile', 'pos')), may hold values from 0 to 2, as said below
- object_real: float32 [2, 256, 2048], P(None, 'pos', 'tile'), may hold values from 0.5 to 1.5
- object_imag: float32 [2, 256, 2048], P(None, 'pos', 'tile'), may hold values from -2 to 2
- probe_real: float32 [128, 128], replicated, may hold values from -6 to 6
- probe_imag: float32 [128, 128], replicated, may hold values from -6 to 6
Outputs:
- grad_real: float32 [2, 256, 2048], P(None, 'pos', 'tile')
- grad_imag: float32 [2, 256, 2048], P(None, 'pos', 'tile')
The draws below stay inside these ranges and needn't reach their ends.
Inputs may be any that keep to these rules, and one draw needn't show every extreme that they name: `coords`: A pattern listed under tile d has its column in [d * 128, (d + 1) * 128); rows are at most 128. `send_slots`: for each block, the live entries over all tiles list each of its 16 patterns exactly once; entries from the count on are arbitrary block-local indices. `send_counts`: for each block the counts sum to 16.
All inputs are finite; a program needn't handle non-finite values.
Results may differ from the reference program's by a relative error of at most 0.018.
Values may be sent and summed in bfloat16 or wider, within the bound.
No kernel may reach another device: no remote copies, remote signals or barrier semaphores. Data moves between devices by JAX's collectives and lax.ppermute only.
A program may use at most 64 MiB of HBM per device.

```python
import math
import jax
import jax.numpy as jnp
from jax import lax

P_SIZE = 128
S = 2
OH = 256
TW = 128
CAP = 2
BLK = 16
NSCAN = 8192
OW = 2048
N_TILE = 16
N_POS = 32


def scan_layout(key):
    sources = N_TILE * N_POS
    slot_total = N_TILE * CAP
    hot_tile = jax.random.randint(jax.random.fold_in(key, 11), (N_POS,), 0, N_TILE)
    hot_source = jnp.tile(hot_tile, N_TILE)
    slot_id = jnp.arange(slot_total, dtype=jnp.int32)
    slot_tile = slot_id // CAP
    random_keys = jax.random.randint(jax.random.fold_in(key, 12), (sources, slot_total), 0, 1 << 20)
    slot_keys = random_keys * slot_total + slot_id[None, :]
    slot_keys = jnp.where(slot_tile[None, :] == hot_source[:, None], slot_id[None, :] - slot_total, slot_keys)
    ordering = jnp.argsort(slot_keys, axis=1)
    slot_rank = jnp.argsort(ordering, axis=1)
    chosen = (slot_rank < BLK).astype(jnp.int32)
    counts = chosen.reshape(sources, N_TILE, CAP).sum(-1).astype(jnp.int32)
    starts = jnp.cumsum(counts, axis=1) - counts
    chosen_keys = jnp.where(chosen == 1, slot_id[None, :], slot_id[None, :] + slot_total)
    chosen_ids = jnp.argsort(chosen_keys, axis=1)[:, :BLK]
    dest_seq = (chosen_ids // CAP).astype(jnp.int32)
    local_ids = jnp.arange(BLK, dtype=jnp.int32)
    shuffle_keys = jax.random.randint(jax.random.fold_in(key, 13), (sources, BLK), 0, 1 << 20) * BLK + local_ids[None, :]
    shuffle = jnp.argsort(shuffle_keys, axis=1).astype(jnp.int32)
    inverse = jnp.argsort(shuffle, axis=1)
    dest_local = jnp.take_along_axis(dest_seq, inverse, axis=1)
    cap_ids = jnp.arange(CAP, dtype=jnp.int32)
    place_idx = starts[:, :, None] + cap_ids[None, None, :]
    live_flag = cap_ids[None, None, :] < counts[:, :, None]
    listed = jnp.take_along_axis(shuffle, jnp.clip(place_idx, 0, BLK - 1).reshape(sources, -1), axis=1)
    listed = listed.reshape(sources, N_TILE, CAP)
    filler = jax.random.randint(jax.random.fold_in(key, 14), (sources, N_TILE, CAP), 0, BLK)
    slot_lists = jnp.where(live_flag, listed, filler).astype(jnp.int32)
    row_draw = jax.random.randint(jax.random.fold_in(key, 15), (sources, BLK), 0, OH - P_SIZE + 1)
    col_draw = dest_local * TW + jax.random.randint(jax.random.fold_in(key, 16), (sources, BLK), 0, TW)
    corner = jnp.stack([row_draw, col_draw], -1).reshape(sources * BLK, 2).astype(jnp.int32)
    return (corner, slot_lists, counts)


def draw_coords(key, part):
    return scan_layout(key)[0]


def draw_send_slots(key, part):
    return scan_layout(key)[1]


def draw_send_counts(key, part):
    return scan_layout(key)[2]


def level_of(rng, dims, cuts, least, top_value):
    def one(axis_at, shards_of):
        draws = jax.random.uniform(jax.random.fold_in(jax.random.fold_in(rng, 6), axis_at), (shards_of,), jnp.float32, least / len(cuts), top_value / len(cuts))
        return jnp.repeat(jnp.exp(draws), dims[axis_at] // shards_of).reshape((-1,) + (1,) * (len(dims) - axis_at - 1))

    loudness = one(*cuts[0])
    for cut in cuts[1:]:
        loudness = loudness * one(*cut)
    return loudness


def bell_draw(own_key, shape, width, limit, pieces=(), kind=jnp.bfloat16):
    drawn = width * jax.random.normal(own_key, shape, jnp.float32)
    if pieces:
        drawn = drawn * level_of(own_key, shape, pieces, -0.22, 0.18)
    return jnp.clip(drawn, -limit, limit).astype(kind)


def setup_inputs(seed: int = 0) -> dict:
    key_of = jax.random.split(jax.random.key(seed), 9)
    patterns = jnp.clip(2.0 * jax.random.uniform(key_of[0], (NSCAN, P_SIZE, P_SIZE), jnp.float32) ** level_of(key_of[0], (NSCAN, P_SIZE, P_SIZE), ((0, 512),), -0.2, 0.2), 0.0, 2.0).astype(jnp.bfloat16)
    coords = draw_coords(jax.random.fold_in(key_of[8], 71), 0)
    send_slots = draw_send_slots(jax.random.fold_in(key_of[8], 71), 0)
    send_counts = draw_send_counts(jax.random.fold_in(key_of[8], 71), 0)
    object_real = jnp.clip(1.0 + 0.1 * jax.random.normal(key_of[4], (S, OH, OW), jnp.float32), 0.5, 1.5)
    object_imag = bell_draw(key_of[5], (S, OH, OW), 0.3, 2.0, ((1, 32), (2, 16)), jnp.float32)
    probe_real = bell_draw(key_of[6], (P_SIZE, P_SIZE), 1.0, 6.0, (), jnp.float32)
    probe_imag = bell_draw(key_of[7], (P_SIZE, P_SIZE), 1.0, 6.0, (), jnp.float32)
    return dict(patterns=patterns, coords=coords, send_slots=send_slots, send_counts=send_counts, object_real=object_real, object_imag=object_imag, probe_real=probe_real, probe_imag=probe_imag)


def build_tables(edge_len):
    indices = jnp.arange(edge_len, dtype=jnp.int32)
    products = indices[:, None] * indices[None, :] % edge_len
    phases = products.astype(jnp.float32) * (2.0 * math.pi / edge_len)
    unit_norm = 1.0 / math.sqrt(edge_len)
    wave_re = jnp.cos(phases) * unit_norm
    wave_im = jnp.sin(phases) * unit_norm
    centred = jnp.where(indices < edge_len // 2, indices, indices - edge_len).astype(jnp.float32)
    chirp = 0.5 * math.pi * centred * centred / edge_len
    kern_re = jnp.cos(chirp)
    kern_im = -jnp.sin(chirp)
    scaled_re = wave_re * kern_re[None, :] - wave_im * kern_im[None, :]
    scaled_im = wave_re * kern_im[None, :] + wave_im * kern_re[None, :]
    highest = lax.Precision.HIGHEST
    fres_re = jnp.dot(scaled_re, wave_re.T, precision=highest) + jnp.dot(scaled_im, wave_im.T, precision=highest)
    fres_im = jnp.dot(scaled_im, wave_re.T, precision=highest) - jnp.dot(scaled_re, wave_im.T, precision=highest)
    fq_re = fres_re.astype(jnp.bfloat16)
    fq_im = fres_im.astype(jnp.bfloat16)
    dft_re = wave_re.astype(jnp.bfloat16)
    dft_im = (-wave_im).astype(jnp.bfloat16)
    return (fq_re, fq_im, fq_re.T, fq_im.T, dft_re, dft_im)

def left_mul(mat_re, mat_im, data_re, data_im):

    def product(a, x):
        return jnp.einsum('jk,nkl->njl', a.astype(jnp.float32), x.astype(jnp.float32))
    return (product(mat_re, data_re) - product(mat_im, data_im), product(mat_re, data_im) + product(mat_im, data_re))

def right_mul(data_re, data_im, mat_re, mat_im):

    def product(x, a):
        return jnp.einsum('njk,kl->njl', x.astype(jnp.float32), a.astype(jnp.float32))
    return (product(data_re, mat_re) - product(data_im, mat_im), product(data_re, mat_im) + product(data_im, mat_re))

def transform(data_re, data_im, left_re, left_im, right_re, right_im):
    half_re, half_im = left_mul(left_re, left_im, data_re, data_im)
    return right_mul(half_re.astype(jnp.bfloat16), half_im.astype(jnp.bfloat16), right_re, right_im)

def slot_gradients(windows, probe_real, probe_imag, measured, weights, tables):
    fq_re, fq_im, fqt_re, fqt_im, dft_re, dft_im = tables
    slices = windows.shape[2]
    shape = (windows.shape[0],) + probe_real.shape
    wave_re = jnp.broadcast_to(probe_real, shape)
    wave_im = jnp.broadcast_to(probe_imag, shape)
    incident = []
    for s in range(slices):
        incident.append((wave_re, wave_im))
        slab_re = windows[:, 0, s]
        slab_im = windows[:, 1, s]
        exit_re = (wave_re * slab_re - wave_im * slab_im).astype(jnp.bfloat16)
        exit_im = (wave_re * slab_im + wave_im * slab_re).astype(jnp.bfloat16)
        if s < slices - 1:
            wave_re, wave_im = transform(exit_re, exit_im, fq_re, fq_im, fqt_re, fqt_im)
        else:
            far_re, far_im = transform(exit_re, exit_im, dft_re, dft_im, dft_re, dft_im)
    excess = far_re * far_re + far_im * far_im - measured.astype(jnp.float32)
    weighted = weights[:, None, None] * excess
    chi_re = (weighted * far_re).astype(jnp.bfloat16)
    chi_im = (weighted * far_im).astype(jnp.bfloat16)
    back_re, back_im = transform(chi_re, chi_im, dft_re, -dft_im, dft_re, -dft_im)
    slice_grads = [None] * slices
    for s in reversed(range(slices)):
        wave_re, wave_im = incident[s]
        slice_grads[s] = (wave_re * back_re + wave_im * back_im, wave_re * back_im - wave_im * back_re)
        if s > 0:
            slab_re = windows[:, 0, s]
            slab_im = windows[:, 1, s]
            carry_re = (slab_re * back_re + slab_im * back_im).astype(jnp.bfloat16)
            carry_im = (slab_re * back_im - slab_im * back_re).astype(jnp.bfloat16)
            back_re, back_im = transform(carry_re, carry_im, fqt_re, -fqt_im, fq_re, -fq_im)
    real_part = jnp.stack([pair[0] for pair in slice_grads], 1)
    imag_part = jnp.stack([pair[1] for pair in slice_grads], 1)
    return jnp.stack([real_part, imag_part], 1)

def reference(patterns, coords, send_slots, send_counts, object_real, object_imag, probe_real, probe_imag):
    tables = build_tables(P_SIZE)
    sources = N_TILE * N_POS
    zero_rim = jnp.zeros((S, OH, P_SIZE), jnp.float32)
    extended = jnp.stack([jnp.concatenate([object_real, zero_rim], 2), jnp.concatenate([object_imag, zero_rim], 2)])
    pattern_blocks = patterns.reshape(sources, BLK, P_SIZE, P_SIZE)
    coord_blocks = coords.reshape(sources, BLK, 2)
    tile_of_slot = jnp.repeat(jnp.arange(N_TILE, dtype=jnp.int32), CAP)
    slot_rank = jnp.tile(jnp.arange(CAP, dtype=jnp.int32), N_TILE)
    anchor = jnp.int32(0)

    def one_block(running, inputs):
        pats, locs, slot_lists, counts = inputs
        listed = slot_lists.reshape(-1)
        measured = pats[listed]
        positions = locs[listed]
        weights = (slot_rank < counts[tile_of_slot]).astype(jnp.float32)
        row_start = jnp.clip(positions[:, 0], 0, OH - P_SIZE).astype(jnp.int32)
        col_start = (tile_of_slot * TW + jnp.clip(positions[:, 1] - tile_of_slot * TW, 0, TW)).astype(jnp.int32)

        def cut_window(r, c):
            return lax.dynamic_slice(extended, (anchor, anchor, r, c), (2, S, P_SIZE, P_SIZE))
        windows = jax.vmap(cut_window)(row_start, col_start)
        slot_terms = slot_gradients(windows, probe_real, probe_imag, measured, weights, tables)

        def add_window(k, summed):
            start = (anchor, anchor, row_start[k], col_start[k])
            current = lax.dynamic_slice(summed, start, (2, S, P_SIZE, P_SIZE))
            return lax.dynamic_update_slice(summed, current + slot_terms[k], start)
        running = lax.fori_loop(0, N_TILE * CAP, add_window, running)
        return (running, None)
    running = jnp.zeros((2, S, OH, OW + P_SIZE), jnp.float32)
    running, _ = lax.scan(one_block, running, (pattern_blocks, coord_blocks, send_slots, send_counts))
    result = running[:, :, :, :OW] * (1.0 / math.sqrt(BLK * N_POS))
    return (result[0], result[1])
```

```python
import functools
import math

import jax
import jax.numpy as jnp
import ml_dtypes
import numpy as np
from jax import lax
from jax.experimental import pallas as pl
from jax.experimental.pallas import tpu as pltpu
from jax.sharding import PartitionSpec as P

BATCH = 4
META_ROWS = 16


def host_tables(edge_len):
    indices = np.arange(edge_len)
    phases = (indices[:, None] * indices[None, :] % edge_len) * (2.0 * math.pi / edge_len)
    wave = np.exp(1j * phases) / math.sqrt(edge_len)
    centred = np.where(indices < edge_len // 2, indices, indices - edge_len)
    kern = np.exp(-0.5j * math.pi * centred * centred / edge_len)
    fresnel = (wave * kern[None, :]) @ wave.conj().T
    fresnel = 0.5 * (fresnel + fresnel.T)

    def rounded(x):
        return x.astype(np.float32).astype(ml_dtypes.bfloat16)

    def left(re, im):
        return np.block([[re, -im], [im, re]])

    def right(re, im):
        return np.block([[re, im], [-im, re]])

    fr, fi = rounded(fresnel.real), rounded(fresnel.imag)
    dr, di = rounded(wave.real), rounded(-wave.imag)
    return np.stack([left(fr, fi), right(fr, fi), left(dr, di), right(dr, di)])


def shifted(value, axis, steps):
    count = lax.axis_size(axis)
    first, last = (max(0, -steps), min(count, count - steps))
    return lax.ppermute(value, axis, [(source, source + steps) for source in range(first, last)])


def pack_kernel(slots, counts, coords, patterns, out, meta, sem, meta_sem, *, n_tile, cap, tile_width, row_max):
    rows = patterns.shape[1]

    def copy(i):
        return pltpu.make_async_copy(
            patterns.at[slots[i]], out.at[i // cap, pl.ds((i % cap) * rows, rows)], sem
        )

    for i in range(n_tile * cap):
        copy(i).start()
    lane = lax.broadcasted_iota(jnp.int32, (META_ROWS, 128), 1)
    for d in range(n_tile):
        value = jnp.zeros((META_ROWS, 128), jnp.int32)
        for c in range(cap):
            j = slots[d * cap + c]
            row = jnp.clip(coords[2 * j], 0, row_max)
            col = jnp.clip(coords[2 * j + 1] - d * tile_width, 0, tile_width)
            live = (c < counts[d]).astype(jnp.int32)
            for k, part in enumerate((row, col, live)):
                value = jnp.where(lane == 3 * c + k, part, value)
        meta[d] = value.astype(jnp.float32).astype(jnp.bfloat16)
    tail = pltpu.make_async_copy(meta, out.at[:, pl.ds(cap * rows, META_ROWS)], meta_sem)
    tail.start()
    for i in range(n_tile * cap):
        copy(i).wait()
    tail.wait()


def pack(patterns, coords, send_slots, send_counts, n_tile, cap, tile_width, row_max):
    rows = patterns.shape[1]
    body = functools.partial(
        pack_kernel, n_tile=n_tile, cap=cap, tile_width=tile_width, row_max=row_max
    )
    return pl.pallas_call(
        body,
        out_shape=jax.ShapeDtypeStruct((n_tile, cap * rows + META_ROWS, 128), jnp.bfloat16),
        in_specs=[
            pl.BlockSpec(memory_space=pltpu.SMEM),
            pl.BlockSpec(memory_space=pltpu.SMEM),
            pl.BlockSpec(memory_space=pltpu.SMEM),
            pl.BlockSpec(memory_space=pl.ANY),
        ],
        out_specs=pl.BlockSpec(memory_space=pl.ANY),
        scratch_shapes=[
            pltpu.VMEM((n_tile, META_ROWS, 128), jnp.bfloat16),
            pltpu.SemaphoreType.DMA,
            pltpu.SemaphoreType.DMA,
        ],
        name="pack",
    )(send_slots, send_counts, coords, patterns)


def grad_kernel(meta, payload, obj, tables, probe, out, slab, acc, order, *, n_tile, cap, n_pos):
    edge = probe.shape[1]
    bf16, f32 = jnp.bfloat16, jnp.float32
    strip = obj.shape[1] // 4
    slot_count = n_tile * cap

    for i in range(slot_count + BATCH):
        order[i] = 0

    def note(i, n):
        live = meta[i // cap, (i % cap) * 3 + 2]

        @pl.when(live > 0)
        def _():
            order[n] = i

        return n + live

    n_live = lax.fori_loop(0, slot_count, note, jnp.int32(0))

    def unpack(p, carry):
        block = obj[p].astype(f32)
        for a in range(4):
            for h in range(2):
                slab[a, h, pl.ds(pl.multiple_of(p * strip, 8), strip), :] = block[
                    a * strip : (a + 1) * strip, h * edge : (h + 1) * edge
                ]
        return carry

    lax.fori_loop(0, n_pos, unpack, 0)
    acc[...] = jnp.zeros(acc.shape, f32)

    lane = lax.broadcasted_iota(jnp.int32, (edge, edge), 1)
    dot = functools.partial(jnp.dot, preferred_element_type=f32)

    def transform(fields, left, right):
        mat_left, mat_right = tables[left], tables[right]
        halves = []
        for k in range(0, len(fields), 2):
            data = jnp.concatenate(
                [jnp.concatenate(pair, axis=0) for pair in fields[k : k + 2]], axis=1
            )
            half = dot(mat_left, data).astype(bf16)
            for h in range(2):
                part = half[:, h * edge : (h + 1) * edge]
                halves.append(jnp.concatenate([part[:edge], part[edge:]], axis=1))
        done = []
        for half in halves:
            full = dot(half, mat_right)
            done.append((full[:, :edge], full[:, edge:]))
        return done

    def times(a, b):
        return (a[0] * b[0] - a[1] * b[1], a[0] * b[1] + a[1] * b[0])

    def conj_times(a, b):
        return (a[0] * b[0] + a[1] * b[1], a[0] * b[1] - a[1] * b[0])

    def rounded(z):
        return (z[0].astype(bf16), z[1].astype(bf16))

    def run_batch(i, carry):
        picks = []
        for b in range(BATCH):
            at = i * BATCH + b
            s = order[at]
            src, c = s // cap, s % cap
            row = meta[src, c * 3]
            col = meta[src, c * 3 + 1]
            weight = (at < n_live).astype(f32)
            picks.append((src, c, row, col, weight, lane >= col))

        def window(b, s):
            _, _, row, _, _, mask = picks[b]
            return tuple(
                jnp.where(
                    mask,
                    slab[part * 2 + s, 0, pl.ds(row, edge), :],
                    slab[part * 2 + s, 1, pl.ds(row, edge), :],
                )
                for part in range(2)
            )

        def rolled_probe(b):
            shift = lax.rem(picks[b][3], edge)
            return (pltpu.roll(probe[0], shift, 1), pltpu.roll(probe[1], shift, 1))

        def add_term(b, s, term):
            _, _, row, _, _, mask = picks[b]
            for part in range(2):
                for h in range(2):
                    piece = jnp.where(mask if h == 0 else ~mask, term[part], 0.0)
                    acc[part * 2 + s, h, pl.ds(row, edge), :] += piece

        exits = [rounded(times(rolled_probe(b), window(b, 0))) for b in range(BATCH)]
        waves = transform(exits, 0, 1)
        exits = [rounded(times(waves[b], window(b, 1))) for b in range(BATCH)]
        far = transform(exits, 2, 3)
        chi = []
        for b in range(BATCH):
            src, c, _, _, weight, _ = picks[b]
            re, im = far[b]
            start = pl.multiple_of(c * edge, edge)
            measured = payload[src, pl.ds(start, edge), :].astype(f32)
            excess = weight * (re * re + im * im - measured)
            chi.append(rounded((excess * re, excess * im)))
        back = transform(chi, 3, 2)
        carried = []
        for b in range(BATCH):
            add_term(b, 1, conj_times(waves[b], back[b]))
            carried.append(rounded(conj_times(window(b, 1), back[b])))
        back = transform(carried, 1, 0)
        for b in range(BATCH):
            add_term(b, 0, conj_times(rolled_probe(b), back[b]))
        return carry

    lax.fori_loop(0, (n_live + BATCH - 1) // BATCH, run_batch, 0)

    def emit(p, carry):
        for a in range(4):
            for h in range(2):
                out[p, a * strip : (a + 1) * strip, h * edge : (h + 1) * edge] = acc[
                    a, h, pl.ds(pl.multiple_of(p * strip, 8), strip), :
                ].astype(bf16)
        return carry

    lax.fori_loop(0, n_pos, emit, 0)


def local_gradient(meta, payload, obj, tables, probe, n_tile, cap, n_pos):
    edge = probe.shape[1]
    rows = n_pos * obj.shape[1] // 4
    body = functools.partial(grad_kernel, n_tile=n_tile, cap=cap, n_pos=n_pos)
    vmem = pl.BlockSpec(memory_space=pltpu.VMEM)
    return pl.pallas_call(
        body,
        out_shape=jax.ShapeDtypeStruct(obj.shape, jnp.bfloat16),
        in_specs=[pl.BlockSpec(memory_space=pltpu.SMEM), vmem, vmem, vmem, vmem],
        out_specs=vmem,
        scratch_shapes=[
            pltpu.VMEM((4, 2, rows, edge), jnp.float32),
            pltpu.VMEM((4, 2, rows, edge), jnp.float32),
            pltpu.SMEM((n_tile * cap + BATCH,), jnp.int32),
        ],
        compiler_params=pltpu.CompilerParams(vmem_limit_bytes=48 * 1024 * 1024),
        name="local_gradient",
    )(meta, payload, obj, tables, probe)


def body(
    patterns, coords, send_slots, send_counts, object_real, object_imag, probe_real, probe_imag
):
    edge_len = probe_real.shape[0]
    slices, strip, tile_width = object_real.shape
    n_tile = lax.axis_size("tile")
    n_pos = lax.axis_size("pos")
    per_source = patterns.shape[0]
    cap = send_slots.shape[2]

    local = jnp.concatenate([object_real, object_imag]).astype(jnp.bfloat16)
    local = local.reshape(2 * slices * strip, tile_width)
    local = jnp.concatenate([local, shifted(local, "tile", -1)], axis=1)
    sent = jnp.broadcast_to(local[None], (n_pos, *local.shape))
    obj = lax.all_to_all(sent, "pos", 0, 0, tiled=True)

    payload = pack(
        patterns,
        coords.reshape(-1),
        send_slots.reshape(-1),
        send_counts.reshape(-1),
        n_tile,
        cap,
        tile_width,
        n_pos * strip - edge_len,
    )
    payload = lax.all_to_all(payload, "tile", 0, 0, tiled=True)
    meta = payload[:, cap * edge_len, :].astype(jnp.int32)

    partial = local_gradient(
        meta,
        payload,
        obj,
        jnp.asarray(host_tables(edge_len)),
        jnp.stack([probe_real, probe_imag]),
        n_tile,
        cap,
        n_pos,
    )
    pieces = lax.all_to_all(partial, "pos", 0, 0, tiled=True)
    share = jnp.sum(pieces.astype(jnp.float32), axis=0)
    share = share * (1.0 / math.sqrt(per_source * n_pos))
    total = share[:, :tile_width] + shifted(share[:, tile_width:], "tile", 1)
    total = total.reshape(2, slices, strip, tile_width)
    return (total[0], total[1])


def solution(mesh):
    in_specs = (
        P(("tile", "pos"), None, None),
        P(("tile", "pos"), None),
        P(("tile", "pos"), None, None),
        P(("tile", "pos"), None),
        P(None, "pos", "tile"),
        P(None, "pos", "tile"),
        P(),
        P(),
    )
    out_specs = (P(None, "pos", "tile"), P(None, "pos", "tile"))
    return jax.shard_map(body, mesh=mesh, in_specs=in_specs, out_specs=out_specs, check_vma=False)
```

```python
import functools
import math

import jax
import jax.numpy as jnp
import ml_dtypes
import numpy as np
from jax import lax
from jax.experimental import pallas as pl
from jax.experimental.pallas import tpu as pltpu
from jax.sharding import PartitionSpec as P

BATCH = 16
CHUNK = 16
META_ROWS = 16


def host_tables(edge_len):
    indices = np.arange(edge_len)
    phases = (indices[:, None] * indices[None, :] % edge_len) * (2.0 * math.pi / edge_len)
    wave = np.exp(1j * phases) / math.sqrt(edge_len)
    centred = np.where(indices < edge_len // 2, indices, indices - edge_len)
    kern = np.exp(-0.5j * math.pi * centred * centred / edge_len)
    fresnel = (wave * kern[None, :]) @ wave.conj().T
    fresnel = 0.5 * (fresnel + fresnel.T)

    def rounded(x):
        return x.astype(np.float32).astype(ml_dtypes.bfloat16)

    def left(re, im):
        return np.block([[re, -im], [im, re]])

    def right(re, im):
        return np.block([[re, im], [-im, re]])

    fr, fi = rounded(fresnel.real), rounded(fresnel.imag)
    dr, di = rounded(wave.real), rounded(-wave.imag)
    return np.stack([left(fr, fi), right(fr, fi), left(dr, di), right(dr, di)])


def pack_kernel(slots, counts, coords, patterns, out, *, n_tile, cap, tile_width, row_max):
    rows = patterns.shape[1]
    lane = lax.broadcasted_iota(jnp.int32, (META_ROWS, 128), 1)
    for d in range(n_tile):
        value = jnp.zeros((META_ROWS, 128), jnp.int32)
        for c in range(cap):
            j = slots[c, d]
            out[d, c * rows : (c + 1) * rows, :] = patterns[j]
            row = jnp.clip(coords[0, j], 0, row_max)
            col = jnp.clip(coords[1, j] - d * tile_width, 0, tile_width)
            live = (c < counts[0, d]).astype(jnp.int32)
            for k, part in enumerate((row, col, live)):
                value = jnp.where(lane == 3 * c + k, part, value)
        out[d, cap * rows :, :] = value.astype(jnp.float32).astype(jnp.bfloat16)


def pack(patterns, coords, send_slots, send_counts, cap, tile_width, row_max):
    rows = patterns.shape[1]
    n_tile = send_counts.shape[1]
    body = functools.partial(
        pack_kernel, n_tile=n_tile, cap=cap, tile_width=tile_width, row_max=row_max
    )
    smem = pl.BlockSpec(memory_space=pltpu.SMEM)
    vmem = pl.BlockSpec(memory_space=pltpu.VMEM)
    return pl.pallas_call(
        body,
        out_shape=jax.ShapeDtypeStruct((n_tile, cap * rows + META_ROWS, 128), jnp.bfloat16),
        in_specs=[smem, smem, smem, vmem],
        out_specs=vmem,
        name="pack",
    )(send_slots, send_counts, coords, patterns)


def grad_kernel(
    here,
    meta,
    payload,
    mine,
    mine_next,
    other,
    other_next,
    tables,
    probe,
    own_out,
    spill_out,
    slab,
    acc,
    order,
    data,
    half,
    field,
    wave,
    rolled,
    *,
    cap,
):
    edge = probe.shape[1]
    bf16, f32 = jnp.bfloat16, jnp.float32
    strip = mine.shape[1] // 4
    slot_count = meta.shape[0] * cap

    for i in range(slot_count + BATCH):
        order[i] = 0

    def note(i, n):
        live = meta[i // cap, (i % cap) * 3 + 2]

        @pl.when(live > 0)
        def _():
            order[n] = i

        return n + live

    n_live = lax.fori_loop(0, slot_count, note, jnp.int32(0))

    def unpack(z, carry):
        for ref, y, h in (
            (mine, here[0], 0),
            (mine_next, here[0], 1),
            (other, 1 - here[0], 0),
            (other_next, 1 - here[0], 1),
        ):
            block = ref[z].astype(f32)
            at = pl.multiple_of((2 * z + y) * strip, 8)
            for a in range(4):
                slab[a, h, pl.ds(at, strip), :] = block[a * strip : (a + 1) * strip]
        return carry

    lax.fori_loop(0, mine.shape[0], unpack, 0, unroll=4)
    acc[...] = jnp.zeros(acc.shape, f32)

    lane = lax.broadcasted_iota(jnp.int32, (CHUNK, edge), 1)
    dot = functools.partial(jnp.dot, preferred_element_type=f32)
    chunks = range(0, edge, CHUNK)

    def transform(left, right):
        for b in range(0, BATCH, 2):
            full = dot(tables[left], data[:, b * edge : (b + 2) * edge]).astype(bf16)
            for h in range(2):
                for k in range(2):
                    half[(b + h) * edge : (b + h + 1) * edge, k * edge : (k + 1) * edge] = full[
                        k * edge : (k + 1) * edge, h * edge : (h + 1) * edge
                    ]

    def finish(right, target):
        for b in range(0, BATCH, 2):
            target[b * edge : (b + 2) * edge, :] = dot(half[b * edge : (b + 2) * edge, :], tables[right])

    def times(a, b):
        return (a[0] * b[0] - a[1] * b[1], a[0] * b[1] + a[1] * b[0])

    def conj_times(a, b):
        return (a[0] * b[0] + a[1] * b[1], a[0] * b[1] - a[1] * b[0])

    def keep(b, r, z):
        for k in range(2):
            data[k * edge + r : k * edge + r + CHUNK, b * edge : (b + 1) * edge] = z[k].astype(bf16)

    def read(ref, b, r):
        at = b * edge + r
        return (ref[at : at + CHUNK, :edge], ref[at : at + CHUNK, edge:])

    def run_batch(i, carry):
        picks = []
        for b in range(BATCH):
            at = i * BATCH + b
            s = order[at]
            src, c = s // cap, s % cap
            row = meta[src, c * 3]
            col = meta[src, c * 3 + 1]
            weight = (at < n_live).astype(f32)
            picks.append((src, c, row, col, weight, lane >= col))

        def window(b, s, r):
            _, _, row, _, _, mask = picks[b]
            return tuple(
                jnp.where(
                    mask,
                    slab[part * 2 + s, 0, pl.ds(row + r, CHUNK), :],
                    slab[part * 2 + s, 1, pl.ds(row + r, CHUNK), :],
                )
                for part in range(2)
            )

        def add_term(b, s, r, term):
            _, _, row, _, _, mask = picks[b]
            for part in range(2):
                for h in range(2):
                    piece = jnp.where(mask, term[part], 0.0) if h == 0 else jnp.where(mask, 0.0, term[part])
                    acc[part * 2 + s, h, pl.ds(row + r, CHUNK), :] += piece

        for b in range(BATCH):
            shift = lax.rem(picks[b][3], edge)
            for r in chunks:
                at = b * edge + r
                re = pltpu.roll(probe[0, r : r + CHUNK, :], shift, 1)
                im = pltpu.roll(probe[1, r : r + CHUNK, :], shift, 1)
                rolled[at : at + CHUNK, :edge] = re
                rolled[at : at + CHUNK, edge:] = im
                keep(b, r, times((re, im), window(b, 0, r)))
        transform(0, 1)
        finish(1, wave)
        for b in range(BATCH):
            for r in chunks:
                keep(b, r, times(read(wave, b, r), window(b, 1, r)))
        transform(2, 3)
        finish(3, field)
        for b in range(BATCH):
            src, c, _, _, weight, _ = picks[b]
            for r in chunks:
                re, im = read(field, b, r)
                start = pl.multiple_of(c * edge + r, CHUNK)
                measured = payload[src, pl.ds(start, CHUNK), :].astype(f32)
                excess = weight * (re * re + im * im - measured)
                keep(b, r, (excess * re, excess * im))
        transform(3, 2)
        finish(2, field)
        for b in range(BATCH):
            for r in chunks:
                back = read(field, b, r)
                add_term(b, 1, r, conj_times(read(wave, b, r), back))
                keep(b, r, conj_times(window(b, 1, r), back))
        transform(1, 0)
        finish(0, field)
        for b in range(BATCH):
            for r in chunks:
                add_term(b, 0, r, conj_times(read(rolled, b, r), read(field, b, r)))
        return carry

    lax.fori_loop(0, (n_live + BATCH - 1) // BATCH, run_batch, 0)

    def emit(p, carry):
        at = pl.multiple_of(p * strip, 8)
        for a in range(4):
            for h, ref in enumerate((own_out, spill_out)):
                ref[p, a * strip : (a + 1) * strip, :] = acc[a, h, pl.ds(at, strip), :].astype(bf16)
        return carry

    lax.fori_loop(0, own_out.shape[0], emit, 0, unroll=4)


def local_gradient(here, meta, payload, strips, tables, probe, cap):
    edge = probe.shape[1]
    n_pos = 2 * strips[0].shape[0]
    rows = n_pos * strips[0].shape[1] // 4
    share = jax.ShapeDtypeStruct((n_pos, *strips[0].shape[1:]), jnp.bfloat16)
    smem = pl.BlockSpec(memory_space=pltpu.SMEM)
    vmem = pl.BlockSpec(memory_space=pltpu.VMEM)
    return pl.pallas_call(
        functools.partial(grad_kernel, cap=cap),
        out_shape=(share, share),
        in_specs=[smem, smem, vmem, vmem, vmem, vmem, vmem, vmem, vmem],
        out_specs=(vmem, vmem),
        scratch_shapes=[
            pltpu.VMEM((4, 2, rows, edge), jnp.float32),
            pltpu.VMEM((4, 2, rows, edge), jnp.float32),
            pltpu.SMEM((meta.shape[0] * cap + BATCH,), jnp.int32),
            pltpu.VMEM((2 * edge, BATCH * edge), jnp.bfloat16),
            pltpu.VMEM((BATCH * edge, 2 * edge), jnp.bfloat16),
            pltpu.VMEM((BATCH * edge, 2 * edge), jnp.float32),
            pltpu.VMEM((BATCH * edge, 2 * edge), jnp.float32),
            pltpu.VMEM((BATCH * edge, 2 * edge), jnp.float32),
        ],
        compiler_params=pltpu.CompilerParams(vmem_limit_bytes=48 * 1024 * 1024),
        name="local_gradient",
    )(here, meta, payload, *strips, tables, probe)


def moved(value, tile_step, flip):
    n_tile, n_pos = lax.axis_size("tile"), lax.axis_size("pos")
    pairs = []
    for t in range(n_tile):
        if 0 <= t + tile_step < n_tile:
            for p in range(n_pos):
                source = (t + tile_step) * n_pos + (p ^ 1 if flip else p)
                pairs.append((source, t * n_pos + p))
    return lax.ppermute(value, ("tile", "pos"), pairs)


def body(
    patterns, coords, send_slots, send_counts, object_real, object_imag, probe_real, probe_imag
):
    edge_len = probe_real.shape[0]
    slices, strip, tile_width = object_real.shape
    n_pos = lax.axis_size("pos")
    per_source = patterns.shape[0]
    cap = send_slots.shape[2]

    local = jnp.concatenate([object_real, object_imag]).astype(jnp.bfloat16)
    local = local.reshape(2 * slices * strip, tile_width)
    sent = jnp.broadcast_to(local[None], (n_pos // 2, *local.shape))
    same_y = [[2 * z + y for z in range(n_pos // 2)] for y in range(2)]
    mine = lax.all_to_all(sent, "pos", 0, 0, axis_index_groups=same_y, tiled=True)

    payload = pack(
        patterns,
        coords.T,
        send_slots[0].T,
        send_counts,
        cap,
        tile_width,
        n_pos * strip - edge_len,
    )
    mine, payload = lax.optimization_barrier((mine, payload))
    strips = (mine, moved(mine, 1, False), moved(mine, 0, True), moved(mine, 1, True))
    payload = lax.all_to_all(payload, "tile", 0, 0, tiled=True)
    meta = payload[:, cap * edge_len, :].astype(jnp.int32)

    own, spill = local_gradient(
        (lax.axis_index("pos") % 2).astype(jnp.int32).reshape(1),
        meta,
        payload,
        strips,
        jnp.asarray(host_tables(edge_len)),
        jnp.stack([probe_real, probe_imag]),
        cap,
    )
    total = own.astype(jnp.float32) + moved(spill, -1, False).astype(jnp.float32)
    pieces = lax.all_to_all(total.astype(jnp.bfloat16), "pos", 0, 0, tiled=True)
    share = jnp.sum(pieces.astype(jnp.float32), axis=0)
    share = share * (1.0 / math.sqrt(per_source * n_pos))
    share = share.reshape(2, slices, strip, tile_width)
    return (share[0], share[1])


def solution(mesh):
    in_specs = (
        P(("tile", "pos"), None, None),
        P(("tile", "pos"), None),
        P(("tile", "pos"), None, None),
        P(("tile", "pos"), None),
        P(None, "pos", "tile"),
        P(None, "pos", "tile"),
        P(),
        P(),
    )
    out_specs = (P(None, "pos", "tile"), P(None, "pos", "tile"))
    return jax.shard_map(body, mesh=mesh, in_specs=in_specs, out_specs=out_specs, check_vma=False)
```

```python
import functools
import math

import jax
import jax.numpy as jnp
import ml_dtypes
import numpy as np
from jax import lax
from jax.experimental import pallas as pl
from jax.experimental.pallas import tpu as pltpu
from jax.sharding import PartitionSpec as P

BATCH = 16
GROUP = 8
SKEW = 1
CHUNK = 16
META_ROWS = 16


def host_tables(edge_len):
    indices = np.arange(edge_len)
    phases = (indices[:, None] * indices[None, :] % edge_len) * (2.0 * math.pi / edge_len)
    wave = np.exp(1j * phases) / math.sqrt(edge_len)
    centred = np.where(indices < edge_len // 2, indices, indices - edge_len)
    kern = np.exp(-0.5j * math.pi * centred * centred / edge_len)
    fresnel = (wave * kern[None, :]) @ wave.conj().T
    fresnel = 0.5 * (fresnel + fresnel.T)

    def rounded(x):
        return x.astype(np.float32).astype(ml_dtypes.bfloat16)

    def left(re, im):
        return np.block([[re, -im], [im, re]])

    def right(re, im):
        return np.block([[re, im], [-im, re]])

    fr, fi = rounded(fresnel.real), rounded(fresnel.imag)
    dr, di = rounded(wave.real), rounded(-wave.imag)
    return np.stack([left(fr, fi), right(fr, fi), left(dr, di), right(dr, di)])


def spread_kernel(real, imag, out):
    parts = [ref[s] for ref in (real, imag) for s in range(real.shape[0])]
    joined = jnp.concatenate(parts, axis=0).astype(jnp.bfloat16)
    for z in range(out.shape[0]):
        out[z] = joined


def spread(real, imag, copies):
    vmem = pl.BlockSpec(memory_space=pltpu.VMEM)
    slices, strip, width = real.shape
    return pl.pallas_call(
        spread_kernel,
        out_shape=jax.ShapeDtypeStruct((copies, 2 * slices * strip, width), jnp.bfloat16),
        in_specs=[vmem, vmem],
        out_specs=vmem,
        name="spread",
    )(real, imag)


def pack_kernel(slots, counts, coords, patterns, out, *, n_tile, cap, tile_width, row_max):
    rows = patterns.shape[1]
    lane = lax.broadcasted_iota(jnp.int32, (META_ROWS, 128), 1)
    for d in range(n_tile):
        value = jnp.zeros((META_ROWS, 128), jnp.int32)
        for c in range(cap):
            j = slots[c, d]
            out[d, c * rows : (c + 1) * rows, :] = patterns[j]
            row = jnp.clip(coords[0, j], 0, row_max)
            col = jnp.clip(coords[1, j] - d * tile_width, 0, tile_width)
            live = (c < counts[0, d]).astype(jnp.int32)
            for k, part in enumerate((row, col, live)):
                value = jnp.where(lane == 3 * c + k, part, value)
        out[d, cap * rows :, :] = value.astype(jnp.float32).astype(jnp.bfloat16)


def pack(patterns, coords, send_slots, send_counts, cap, tile_width, row_max):
    rows = patterns.shape[1]
    n_tile = send_counts.shape[1]
    body = functools.partial(
        pack_kernel, n_tile=n_tile, cap=cap, tile_width=tile_width, row_max=row_max
    )
    smem = pl.BlockSpec(memory_space=pltpu.SMEM)
    vmem = pl.BlockSpec(memory_space=pltpu.VMEM)
    return pl.pallas_call(
        body,
        out_shape=jax.ShapeDtypeStruct((n_tile, cap * rows + META_ROWS, 128), jnp.bfloat16),
        in_specs=[smem, smem, smem, vmem],
        out_specs=vmem,
        name="pack",
    )(send_slots, send_counts, coords, patterns)


def grad_kernel(
    here,
    meta,
    payload,
    mine,
    mine_next,
    other,
    other_next,
    tables,
    probe,
    own_out,
    spill_out,
    slab,
    acc,
    order,
    data,
    half,
    field,
    wave,
    rolled,
    cut,
    *,
    cap,
):
    edge = probe.shape[1]
    bf16, f32 = jnp.bfloat16, jnp.float32
    strip = mine.shape[1] // 4
    slot_count = meta.shape[0] * cap

    for i in range(slot_count + BATCH):
        order[i] = 0

    def note(i, n):
        live = meta[i // cap, (i % cap) * 3 + 2]

        @pl.when(live > 0)
        def _():
            order[n] = i

        return n + live

    n_live = lax.fori_loop(0, slot_count, note, jnp.int32(0))

    def unpack(z, carry):
        for ref, y, h in (
            (mine, here[0], 0),
            (mine_next, here[0], 1),
            (other, 1 - here[0], 0),
            (other_next, 1 - here[0], 1),
        ):
            block = ref[z].astype(f32)
            at = pl.multiple_of((2 * z + y) * strip, 8)
            for a in range(4):
                slab[a, h, pl.ds(at, strip), :] = block[a * strip : (a + 1) * strip]
        return carry

    lax.fori_loop(0, mine.shape[0], unpack, 0, unroll=4)
    acc[...] = jnp.zeros(acc.shape, f32)

    lane = lax.broadcasted_iota(jnp.int32, (CHUNK, edge), 1)
    dot = functools.partial(jnp.dot, preferred_element_type=f32)
    chunks = range(0, edge, CHUNK)

    def apply_left(group, left):
        for b in range(group * GROUP, (group + 1) * GROUP, 2):
            full = dot(tables[left], data[:, b * edge : (b + 2) * edge]).astype(bf16)
            for h in range(2):
                for k in range(2):
                    half[(b + h) * edge : (b + h + 1) * edge, k * edge : (k + 1) * edge] = full[
                        k * edge : (k + 1) * edge, h * edge : (h + 1) * edge
                    ]

    def apply_right(group, right, target):
        at = group * GROUP * edge
        target[at : at + GROUP * edge, :] = dot(half[at : at + GROUP * edge, :], tables[right])

    def times(a, b):
        return (a[0] * b[0] - a[1] * b[1], a[0] * b[1] + a[1] * b[0])

    def conj_times(a, b):
        return (a[0] * b[0] + a[1] * b[1], a[0] * b[1] - a[1] * b[0])

    def keep(b, r, z):
        for k in range(2):
            data[k * edge + r : k * edge + r + CHUNK, b * edge : (b + 1) * edge] = z[k].astype(bf16)

    def read(ref, b, r):
        at = b * edge + r
        return (ref[at : at + CHUNK, :edge], ref[at : at + CHUNK, edge:])

    def members(group):
        return range(group * GROUP, (group + 1) * GROUP)

    def run_batch(i, carry):
        picks = []
        for b in range(BATCH):
            at = i * BATCH + b
            s = order[at]
            src, c = s // cap, s % cap
            row = meta[src, c * 3]
            col = meta[src, c * 3 + 1]
            weight = (at < n_live).astype(f32)
            picks.append((src, c, row, col, weight, lane >= col))

        def window(b, s, r):
            _, _, row, _, _, mask = picks[b]
            return tuple(
                jnp.where(
                    mask,
                    slab[part * 2 + s, 0, pl.ds(row + r, CHUNK), :],
                    slab[part * 2 + s, 1, pl.ds(row + r, CHUNK), :],
                )
                for part in range(2)
            )

        def add_term(b, s, r, term):
            _, _, row, _, _, mask = picks[b]
            for part in range(2):
                for h in range(2):
                    spot = acc.at[part * 2 + s, h, pl.ds(row + r, CHUNK), :]
                    pltpu.store(spot, spot[...] + term[part], mask=mask if h == 0 else ~mask)

        def enter(group):
            for b in members(group):
                shift = lax.rem(picks[b][3], edge)
                for r in chunks:
                    at = b * edge + r
                    re = pltpu.roll(probe[0, r : r + CHUNK, :], shift, 1)
                    im = pltpu.roll(probe[1, r : r + CHUNK, :], shift, 1)
                    rolled[at : at + CHUNK, :edge] = re
                    rolled[at : at + CHUNK, edge:] = im
                    keep(b, r, times((re, im), window(b, 0, r)))

        def leave(group):
            for b in members(group):
                for r in chunks:
                    at = b * edge + r
                    slab_part = window(b, 1, r)
                    cut[at : at + CHUNK, :edge] = slab_part[0]
                    cut[at : at + CHUNK, edge:] = slab_part[1]
                    keep(b, r, times(read(wave, b, r), slab_part))

        def compare(group):
            for b in members(group):
                src, c, _, _, weight, _ = picks[b]
                for r in chunks:
                    re, im = read(field, b, r)
                    start = pl.multiple_of(c * edge + r, CHUNK)
                    measured = payload[src, pl.ds(start, CHUNK), :].astype(f32)
                    excess = weight * (re * re + im * im - measured)
                    keep(b, r, (excess * re, excess * im))

        def turn(group):
            for b in members(group):
                for r in chunks:
                    back = read(field, b, r)
                    add_term(b, 1, r, conj_times(read(wave, b, r), back))
                    keep(b, r, conj_times(read(cut, b, r), back))

        def close(group):
            for b in members(group):
                for r in chunks:
                    add_term(b, 0, r, conj_times(read(rolled, b, r), read(field, b, r)))

        steps = (
            enter,
            lambda g: apply_left(g, 0),
            lambda g: apply_right(g, 1, wave),
            leave,
            lambda g: apply_left(g, 2),
            lambda g: apply_right(g, 3, field),
            compare,
            lambda g: apply_left(g, 3),
            lambda g: apply_right(g, 2, field),
            turn,
            lambda g: apply_left(g, 1),
            lambda g: apply_right(g, 0, field),
            close,
        )
        n_groups = BATCH // GROUP
        for t in range(len(steps) + (n_groups - 1) * SKEW):
            for g in range(n_groups):
                if 0 <= t - g * SKEW < len(steps):
                    steps[t - g * SKEW](g)
        return carry

    lax.fori_loop(0, (n_live + BATCH - 1) // BATCH, run_batch, 0)

    def emit(p, carry):
        at = pl.multiple_of(p * strip, 8)
        for a in range(4):
            for h, ref in enumerate((own_out, spill_out)):
                ref[p, a * strip : (a + 1) * strip, :] = acc[a, h, pl.ds(at, strip), :].astype(bf16)
        return carry

    lax.fori_loop(0, own_out.shape[0], emit, 0, unroll=4)


def local_gradient(here, meta, payload, strips, tables, probe, cap):
    edge = probe.shape[1]
    n_pos = 2 * strips[0].shape[0]
    rows = n_pos * strips[0].shape[1] // 4
    share = jax.ShapeDtypeStruct((n_pos, *strips[0].shape[1:]), jnp.bfloat16)
    smem = pl.BlockSpec(memory_space=pltpu.SMEM)
    vmem = pl.BlockSpec(memory_space=pltpu.VMEM)
    return pl.pallas_call(
        functools.partial(grad_kernel, cap=cap),
        out_shape=(share, share),
        in_specs=[smem, smem, vmem, vmem, vmem, vmem, vmem, vmem, vmem],
        out_specs=(vmem, vmem),
        scratch_shapes=[
            pltpu.VMEM((4, 2, rows, edge), jnp.float32),
            pltpu.VMEM((4, 2, rows, edge), jnp.float32),
            pltpu.SMEM((meta.shape[0] * cap + BATCH,), jnp.int32),
            pltpu.VMEM((2 * edge, BATCH * edge), jnp.bfloat16),
            pltpu.VMEM((BATCH * edge, 2 * edge), jnp.bfloat16),
            pltpu.VMEM((BATCH * edge, 2 * edge), jnp.float32),
            pltpu.VMEM((BATCH * edge, 2 * edge), jnp.float32),
            pltpu.VMEM((BATCH * edge, 2 * edge), jnp.float32),
            pltpu.VMEM((BATCH * edge, 2 * edge), jnp.float32),
        ],
        compiler_params=pltpu.CompilerParams(vmem_limit_bytes=48 * 1024 * 1024),
        name="local_gradient",
    )(here, meta, payload, *strips, tables, probe)


def moved(value, tile_step, flip):
    n_tile, n_pos = lax.axis_size("tile"), lax.axis_size("pos")
    pairs = []
    for t in range(n_tile):
        if 0 <= t + tile_step < n_tile:
            for p in range(n_pos):
                source = (t + tile_step) * n_pos + (p ^ 1 if flip else p)
                pairs.append((source, t * n_pos + p))
    return lax.ppermute(value, ("tile", "pos"), pairs)


def body(
    patterns, coords, send_slots, send_counts, object_real, object_imag, probe_real, probe_imag
):
    edge_len = probe_real.shape[0]
    slices, strip, tile_width = object_real.shape
    n_pos = lax.axis_size("pos")
    per_source = patterns.shape[0]
    cap = send_slots.shape[2]

    sent = spread(object_real, object_imag, n_pos // 2)
    same_y = [[2 * z + y for z in range(n_pos // 2)] for y in range(2)]
    mine = lax.all_to_all(sent, "pos", 0, 0, axis_index_groups=same_y, tiled=True)

    payload = pack(
        patterns,
        coords.T,
        send_slots[0].T,
        send_counts,
        cap,
        tile_width,
        n_pos * strip - edge_len,
    )
    mine, payload = lax.optimization_barrier((mine, payload))
    strips = (mine, moved(mine, 1, False), moved(mine, 0, True), moved(mine, 1, True))
    payload = lax.all_to_all(payload, "tile", 0, 0, tiled=True)
    meta = payload[:, cap * edge_len, :].astype(jnp.int32)

    own, spill = local_gradient(
        (lax.axis_index("pos") % 2).astype(jnp.int32).reshape(1),
        meta,
        payload,
        strips,
        jnp.asarray(host_tables(edge_len)),
        jnp.stack([probe_real, probe_imag]),
        cap,
    )
    total = own.astype(jnp.float32) + moved(spill, -1, False).astype(jnp.float32)
    pieces = lax.all_to_all(total.astype(jnp.bfloat16), "pos", 0, 0, tiled=True)
    share = jnp.sum(pieces.astype(jnp.float32), axis=0)
    share = share * (1.0 / math.sqrt(per_source * n_pos))
    share = share.reshape(2, slices, strip, tile_width)
    return (share[0], share[1])


def solution(mesh):
    in_specs = (
        P(("tile", "pos"), None, None),
        P(("tile", "pos"), None),
        P(("tile", "pos"), None, None),
        P(("tile", "pos"), None),
        P(None, "pos", "tile"),
        P(None, "pos", "tile"),
        P(),
        P(),
    )
    out_specs = (P(None, "pos", "tile"), P(None, "pos", "tile"))
    return jax.shard_map(body, mesh=mesh, in_specs=in_specs, out_specs=out_specs, check_vma=False)
```

```python
import functools
import math

import jax
import jax.numpy as jnp
import ml_dtypes
import numpy as np
from jax import lax
from jax.experimental import pallas as pl
from jax.experimental.pallas import tpu as pltpu
from jax.sharding import PartitionSpec as P

BATCH = 16
GROUP = 8
SKEW = 1
CHUNK = 16
META_ROWS = 16


def host_tables(edge_len):
    indices = np.arange(edge_len)
    phases = (indices[:, None] * indices[None, :] % edge_len) * (2.0 * math.pi / edge_len)
    wave = np.exp(1j * phases) / math.sqrt(edge_len)
    centred = np.where(indices < edge_len // 2, indices, indices - edge_len)
    kern = np.exp(-0.5j * math.pi * centred * centred / edge_len)
    fresnel = (wave * kern[None, :]) @ wave.conj().T
    fresnel = 0.5 * (fresnel + fresnel.T)

    def rounded(x):
        return x.astype(np.float32).astype(ml_dtypes.bfloat16)

    def left(re, im):
        return np.block([[re, -im], [im, re]])

    def right(re, im):
        return np.block([[re, im], [-im, re]])

    fr, fi = rounded(fresnel.real), rounded(fresnel.imag)
    dr, di = rounded(wave.real), rounded(-wave.imag)
    return np.stack([left(fr, fi), right(fr, fi), left(dr, di), right(dr, di)])


def spread_kernel(real, imag, out):
    parts = [ref[s] for ref in (real, imag) for s in range(real.shape[0])]
    joined = jnp.concatenate(parts, axis=0).astype(jnp.bfloat16)
    for z in range(out.shape[0]):
        out[z] = joined


def spread(real, imag, copies):
    vmem = pl.BlockSpec(memory_space=pltpu.VMEM)
    slices, strip, width = real.shape
    return pl.pallas_call(
        spread_kernel,
        out_shape=jax.ShapeDtypeStruct((copies, 2 * slices * strip, width), jnp.bfloat16),
        in_specs=[vmem, vmem],
        out_specs=vmem,
        name="spread",
    )(real, imag)


def pack_kernel(slots, counts, coords, patterns, out, *, n_tile, cap, tile_width, row_max):
    rows = patterns.shape[1]
    lane = lax.broadcasted_iota(jnp.int32, (META_ROWS, 128), 1)
    for d in range(n_tile):
        value = jnp.zeros((META_ROWS, 128), jnp.int32)
        for c in range(cap):
            j = slots[c, d]
            out[d, c * rows : (c + 1) * rows, :] = patterns[j]
            row = jnp.clip(coords[0, j], 0, row_max)
            col = jnp.clip(coords[1, j] - d * tile_width, 0, tile_width)
            live = (c < counts[0, d]).astype(jnp.int32)
            for k, part in enumerate((row, col, live)):
                value = jnp.where(lane == 3 * c + k, part, value)
        out[d, cap * rows :, :] = value.astype(jnp.float32).astype(jnp.bfloat16)


def pack(patterns, coords, send_slots, send_counts, cap, tile_width, row_max):
    rows = patterns.shape[1]
    n_tile = send_counts.shape[1]
    body = functools.partial(
        pack_kernel, n_tile=n_tile, cap=cap, tile_width=tile_width, row_max=row_max
    )
    smem = pl.BlockSpec(memory_space=pltpu.SMEM)
    vmem = pl.BlockSpec(memory_space=pltpu.VMEM)
    return pl.pallas_call(
        body,
        out_shape=jax.ShapeDtypeStruct((n_tile, cap * rows + META_ROWS, 128), jnp.bfloat16),
        in_specs=[smem, smem, smem, vmem],
        out_specs=vmem,
        name="pack",
    )(send_slots, send_counts, coords, patterns)


def grad_kernel(
    here,
    meta,
    payload,
    mine,
    mine_next,
    other,
    other_next,
    tables,
    probe,
    own_out,
    spill_out,
    slab,
    acc,
    order,
    data,
    half,
    field,
    wave,
    rolled,
    cut,
    *,
    cap,
):
    edge = probe.shape[1]
    bf16, f32 = jnp.bfloat16, jnp.float32
    strip = mine.shape[1] // 4
    slot_count = meta.shape[0] * cap

    for i in range(slot_count + BATCH):
        order[i] = 0

    def note(i, n):
        live = meta[i // cap, (i % cap) * 3 + 2]

        @pl.when(live > 0)
        def _():
            order[n] = i

        return n + live

    n_live = lax.fori_loop(0, slot_count, note, jnp.int32(0))

    def unpack(z, carry):
        for ref, y, h in (
            (mine, here[0], 0),
            (mine_next, here[0], 1),
            (other, 1 - here[0], 0),
            (other_next, 1 - here[0], 1),
        ):
            block = ref[z].astype(f32)
            at = pl.multiple_of((2 * z + y) * strip, 8)
            for a in range(4):
                slab[a, h, pl.ds(at, strip), :] = block[a * strip : (a + 1) * strip]
        return carry

    lax.fori_loop(0, mine.shape[0], unpack, 0, unroll=4)
    acc[...] = jnp.zeros(acc.shape, f32)

    lane = lax.broadcasted_iota(jnp.int32, (CHUNK, edge), 1)
    dot = functools.partial(jnp.dot, preferred_element_type=f32)
    chunks = range(0, edge, CHUNK)

    def apply_left(group, left):
        for b in range(group * GROUP, (group + 1) * GROUP, 2):
            full = dot(tables[left], data[:, b * edge : (b + 2) * edge]).astype(bf16)
            for h in range(2):
                for k in range(2):
                    half[(b + h) * edge : (b + h + 1) * edge, k * edge : (k + 1) * edge] = full[
                        k * edge : (k + 1) * edge, h * edge : (h + 1) * edge
                    ]

    def apply_right(group, right, target):
        at = group * GROUP * edge
        target[at : at + GROUP * edge, :] = dot(half[at : at + GROUP * edge, :], tables[right])

    def times(a, b):
        return (a[0] * b[0] - a[1] * b[1], a[0] * b[1] + a[1] * b[0])

    def conj_times(a, b):
        return (a[0] * b[0] + a[1] * b[1], a[0] * b[1] - a[1] * b[0])

    def keep(b, r, z):
        for k in range(2):
            data[k * edge + r : k * edge + r + CHUNK, b * edge : (b + 1) * edge] = z[k].astype(bf16)

    def read(ref, b, r):
        at = b * edge + r
        return (ref[at : at + CHUNK, :edge], ref[at : at + CHUNK, edge:])

    def members(group):
        return range(group * GROUP, (group + 1) * GROUP)

    def run_batch(i, carry):
        picks = []
        for b in range(BATCH):
            at = i * BATCH + b
            s = order[at]
            src, c = s // cap, s % cap
            row = meta[src, c * 3]
            col = meta[src, c * 3 + 1]
            weight = (at < n_live).astype(f32)
            picks.append((src, c, row, col, weight, lane >= col))

        def window(b, s, r):
            _, _, row, _, _, mask = picks[b]
            return tuple(
                jnp.where(
                    mask,
                    slab[part * 2 + s, 0, pl.ds(row + r, CHUNK), :],
                    slab[part * 2 + s, 1, pl.ds(row + r, CHUNK), :],
                )
                for part in range(2)
            )

        def add_term(b, s, r, term):
            _, _, row, _, _, mask = picks[b]
            for part in range(2):
                for h in range(2):
                    spot = acc.at[part * 2 + s, h, pl.ds(row + r, CHUNK), :]
                    pltpu.store(spot, spot[...] + term[part], mask=mask if h == 0 else ~mask)

        def enter(group):
            for b in members(group):
                shift = lax.rem(picks[b][3], edge)
                for r in chunks:
                    at = b * edge + r
                    re = pltpu.roll(probe[0, r : r + CHUNK, :], shift, 1)
                    im = pltpu.roll(probe[1, r : r + CHUNK, :], shift, 1)
                    rolled[at : at + CHUNK, :edge] = re
                    rolled[at : at + CHUNK, edge:] = im
                    keep(b, r, times((re, im), window(b, 0, r)))

        def leave(group):
            for b in members(group):
                for r in chunks:
                    at = b * edge + r
                    slab_part = window(b, 1, r)
                    cut[at : at + CHUNK, :edge] = slab_part[0]
                    cut[at : at + CHUNK, edge:] = slab_part[1]
                    keep(b, r, times(read(wave, b, r), slab_part))

        def compare(group):
            for b in members(group):
                src, c, _, _, weight, _ = picks[b]
                for r in chunks:
                    re, im = read(field, b, r)
                    start = pl.multiple_of(c * edge + r, CHUNK)
                    measured = payload[src, pl.ds(start, CHUNK), :].astype(f32)
                    excess = weight * (re * re + im * im - measured)
                    keep(b, r, (excess * re, excess * im))

        def turn(group):
            for b in members(group):
                for r in chunks:
                    back = read(field, b, r)
                    add_term(b, 1, r, conj_times(read(wave, b, r), back))
                    keep(b, r, conj_times(read(cut, b, r), back))

        def close(group):
            for b in members(group):
                for r in chunks:
                    add_term(b, 0, r, conj_times(read(rolled, b, r), read(field, b, r)))

        steps = (
            enter,
            lambda g: apply_left(g, 0),
            lambda g: apply_right(g, 1, wave),
            leave,
            lambda g: apply_left(g, 2),
            lambda g: apply_right(g, 3, field),
            compare,
            lambda g: apply_left(g, 3),
            lambda g: apply_right(g, 2, field),
            turn,
            lambda g: apply_left(g, 1),
            lambda g: apply_right(g, 0, field),
            close,
        )
        n_groups = BATCH // GROUP
        for t in range(len(steps) + (n_groups - 1) * SKEW):
            for g in range(n_groups):
                if 0 <= t - g * SKEW < len(steps):
                    steps[t - g * SKEW](g)
        return carry

    lax.fori_loop(0, (n_live + BATCH - 1) // BATCH, run_batch, 0)

    def emit(p, carry):
        at = pl.multiple_of(p * strip, 8)
        for a in range(4):
            for h, ref in enumerate((own_out, spill_out)):
                ref[p, a * strip : (a + 1) * strip, :] = acc[a, h, pl.ds(at, strip), :].astype(bf16)
        return carry

    lax.fori_loop(0, own_out.shape[0], emit, 0, unroll=4)


def local_gradient(here, meta, payload, strips, tables, probe, cap):
    edge = probe.shape[1]
    n_pos = 2 * strips[0].shape[0]
    rows = n_pos * strips[0].shape[1] // 4
    share = jax.ShapeDtypeStruct((n_pos, *strips[0].shape[1:]), jnp.bfloat16)
    smem = pl.BlockSpec(memory_space=pltpu.SMEM)
    vmem = pl.BlockSpec(memory_space=pltpu.VMEM)
    return pl.pallas_call(
        functools.partial(grad_kernel, cap=cap),
        out_shape=(share, share),
        in_specs=[smem, smem, vmem, vmem, vmem, vmem, vmem, vmem, vmem],
        out_specs=(vmem, vmem),
        scratch_shapes=[
            pltpu.VMEM((4, 2, rows, edge), jnp.float32),
            pltpu.VMEM((4, 2, rows, edge), jnp.float32),
            pltpu.SMEM((meta.shape[0] * cap + BATCH,), jnp.int32),
            pltpu.VMEM((2 * edge, BATCH * edge), jnp.bfloat16),
            pltpu.VMEM((BATCH * edge, 2 * edge), jnp.bfloat16),
            pltpu.VMEM((BATCH * edge, 2 * edge), jnp.float32),
            pltpu.VMEM((BATCH * edge, 2 * edge), jnp.float32),
            pltpu.VMEM((BATCH * edge, 2 * edge), jnp.float32),
            pltpu.VMEM((BATCH * edge, 2 * edge), jnp.float32),
        ],
        compiler_params=pltpu.CompilerParams(vmem_limit_bytes=48 * 1024 * 1024),
        name="local_gradient",
    )(here, meta, payload, *strips, tables, probe)


def moved(value, tile_step, flip):
    n_tile, n_pos = lax.axis_size("tile"), lax.axis_size("pos")
    pairs = []
    for t in range(n_tile):
        if 0 <= t + tile_step < n_tile:
            for p in range(n_pos):
                source = (t + tile_step) * n_pos + (p ^ 1 if flip else p)
                pairs.append((source, t * n_pos + p))
    return lax.ppermute(value, ("tile", "pos"), pairs)


def body(
    patterns, coords, send_slots, send_counts, object_real, object_imag, probe_real, probe_imag
):
    edge_len = probe_real.shape[0]
    slices, strip, tile_width = object_real.shape
    n_pos = lax.axis_size("pos")
    per_source = patterns.shape[0]
    cap = send_slots.shape[2]

    sent = spread(object_real, object_imag, n_pos // 2)
    same_y = [[2 * z + y for z in range(n_pos // 2)] for y in range(2)]
    mine = lax.all_to_all(sent, "pos", 0, 0, axis_index_groups=same_y, tiled=True)

    payload = pack(
        patterns,
        coords.T,
        send_slots[0].T,
        send_counts,
        cap,
        tile_width,
        n_pos * strip - edge_len,
    )
    other = moved(mine, 0, True)
    other, payload = lax.optimization_barrier((other, payload))
    strips = (mine, moved(mine, 1, False), other, moved(other, 1, False))
    payload = lax.all_to_all(payload, "tile", 0, 0, tiled=True)
    meta = payload[:, cap * edge_len, :].astype(jnp.int32)

    own, spill = local_gradient(
        (lax.axis_index("pos") % 2).astype(jnp.int32).reshape(1),
        meta,
        payload,
        strips,
        jnp.asarray(host_tables(edge_len)),
        jnp.stack([probe_real, probe_imag]),
        cap,
    )
    total = own.astype(jnp.float32) + moved(spill, -1, False).astype(jnp.float32)
    pieces = lax.all_to_all(total.astype(jnp.bfloat16), "pos", 0, 0, tiled=True)
    share = jnp.sum(pieces.astype(jnp.float32), axis=0)
    share = share * (1.0 / math.sqrt(per_source * n_pos))
    share = share.reshape(2, slices, strip, tile_width)
    return (share[0], share[1])


def solution(mesh):
    in_specs = (
        P(("tile", "pos"), None, None),
        P(("tile", "pos"), None),
        P(("tile", "pos"), None, None),
        P(("tile", "pos"), None),
        P(None, "pos", "tile"),
        P(None, "pos", "tile"),
        P(),
        P(),
    )
    out_specs = (P(None, "pos", "tile"), P(None, "pos", "tile"))
    return jax.shard_map(body, mesh=mesh, in_specs=in_specs, out_specs=out_specs, check_vma=False)
```

```python
import functools
import math

import jax
import jax.numpy as jnp
import ml_dtypes
import numpy as np
from jax import lax
from jax.experimental import pallas as pl
from jax.experimental.pallas import tpu as pltpu
from jax.sharding import PartitionSpec as P

BATCH = 16
GROUP = 8
SKEW = 1
CHUNK = 16
META_ROWS = 16


def host_tables(edge_len):
    indices = np.arange(edge_len)
    phases = (indices[:, None] * indices[None, :] % edge_len) * (2.0 * math.pi / edge_len)
    wave = np.exp(1j * phases) / math.sqrt(edge_len)
    centred = np.where(indices < edge_len // 2, indices, indices - edge_len)
    kern = np.exp(-0.5j * math.pi * centred * centred / edge_len)
    fresnel = (wave * kern[None, :]) @ wave.conj().T
    fresnel = 0.5 * (fresnel + fresnel.T)

    def rounded(x):
        return x.astype(np.float32).astype(ml_dtypes.bfloat16)

    def left(re, im):
        return np.block([[re, -im], [im, re]])

    def right(re, im):
        return np.block([[re, im], [-im, re]])

    fr, fi = rounded(fresnel.real), rounded(fresnel.imag)
    dr, di = rounded(wave.real), rounded(-wave.imag)
    return np.stack([left(fr, fi), right(fr, fi), left(dr, di), right(dr, di)])


def spread_kernel(real, imag, out):
    parts = [ref[s] for ref in (real, imag) for s in range(real.shape[0])]
    joined = jnp.concatenate(parts, axis=0).astype(jnp.bfloat16)
    for z in range(out.shape[0]):
        out[z] = joined


def spread(real, imag, copies):
    vmem = pl.BlockSpec(memory_space=pltpu.VMEM)
    slices, strip, width = real.shape
    return pl.pallas_call(
        spread_kernel,
        out_shape=jax.ShapeDtypeStruct((copies, 2 * slices * strip, width), jnp.bfloat16),
        in_specs=[vmem, vmem],
        out_specs=vmem,
        name="spread",
    )(real, imag)


def pack_kernel(slots, counts, coords, patterns, out, *, n_tile, cap, tile_width, row_max):
    rows = patterns.shape[1]
    lane = lax.broadcasted_iota(jnp.int32, (META_ROWS, 128), 1)
    for d in range(n_tile):
        value = jnp.zeros((META_ROWS, 128), jnp.int32)
        for c in range(cap):
            j = slots[c, d]
            out[d, c * rows : (c + 1) * rows, :] = patterns[j]
            row = jnp.clip(coords[0, j], 0, row_max)
            col = jnp.clip(coords[1, j] - d * tile_width, 0, tile_width)
            live = (c < counts[0, d]).astype(jnp.int32)
            for k, part in enumerate((row, col, live)):
                value = jnp.where(lane == 3 * c + k, part, value)
        out[d, cap * rows :, :] = value.astype(jnp.float32).astype(jnp.bfloat16)


def pack(patterns, coords, send_slots, send_counts, cap, tile_width, row_max):
    rows = patterns.shape[1]
    n_tile = send_counts.shape[1]
    body = functools.partial(
        pack_kernel, n_tile=n_tile, cap=cap, tile_width=tile_width, row_max=row_max
    )
    smem = pl.BlockSpec(memory_space=pltpu.SMEM)
    vmem = pl.BlockSpec(memory_space=pltpu.VMEM)
    return pl.pallas_call(
        body,
        out_shape=jax.ShapeDtypeStruct((n_tile, cap * rows + META_ROWS, 128), jnp.bfloat16),
        in_specs=[smem, smem, smem, vmem],
        out_specs=vmem,
        name="pack",
    )(send_slots, send_counts, coords, patterns)


def grad_kernel(
    here,
    meta,
    payload,
    mine,
    other,
    other_next,
    mine_next,
    tables,
    probe,
    own_out,
    spill_out,
    slab,
    acc,
    order,
    data,
    half,
    field,
    wave,
    rolled,
    cut,
    *,
    cap,
):
    edge = probe.shape[1]
    bf16, f32 = jnp.bfloat16, jnp.float32
    strip = mine.shape[1] // 4
    slot_count = meta.shape[0] * cap

    for i in range(slot_count + BATCH):
        order[i] = 0

    n_live = jnp.int32(0)
    for i in range(slot_count):
        order[n_live] = i
        n_live += meta[i // cap, (i % cap) * 3 + 2]

    def unpack(z, carry):
        for ref, y, h in (
            (mine, here[0], 0),
            (mine_next, here[0], 1),
            (other, 1 - here[0], 0),
            (other_next, 1 - here[0], 1),
        ):
            block = ref[z].astype(f32)
            at = pl.multiple_of((2 * z + y) * strip, 8)
            for a in range(4):
                slab[a, h, pl.ds(at, strip), :] = block[a * strip : (a + 1) * strip]
        return carry

    lax.fori_loop(0, mine.shape[0], unpack, 0, unroll=4)
    acc[...] = jnp.zeros(acc.shape, f32)

    lane = lax.broadcasted_iota(jnp.int32, (CHUNK, edge), 1)
    dot = functools.partial(jnp.dot, preferred_element_type=f32)
    chunks = range(0, edge, CHUNK)

    def apply_left(group, left):
        for b in range(group * GROUP, (group + 1) * GROUP, 2):
            full = dot(tables[left], data[:, b * edge : (b + 2) * edge]).astype(bf16)
            for h in range(2):
                for k in range(2):
                    half[(b + h) * edge : (b + h + 1) * edge, k * edge : (k + 1) * edge] = full[
                        k * edge : (k + 1) * edge, h * edge : (h + 1) * edge
                    ]

    def apply_right(group, right, target):
        at = group * GROUP * edge
        target[at : at + GROUP * edge, :] = dot(half[at : at + GROUP * edge, :], tables[right])

    def times(a, b):
        return (a[0] * b[0] - a[1] * b[1], a[0] * b[1] + a[1] * b[0])

    def conj_times(a, b):
        return (a[0] * b[0] + a[1] * b[1], a[0] * b[1] - a[1] * b[0])

    def keep(b, r, z):
        for k in range(2):
            data[k * edge + r : k * edge + r + CHUNK, b * edge : (b + 1) * edge] = z[k].astype(bf16)

    def read(ref, b, r):
        at = b * edge + r
        return (ref[at : at + CHUNK, :edge], ref[at : at + CHUNK, edge:])

    def members(group):
        return range(group * GROUP, (group + 1) * GROUP)

    def run_batch(i, carry):
        picks = []
        for b in range(BATCH):
            at = i * BATCH + b
            s = order[at]
            src, c = s // cap, s % cap
            row = meta[src, c * 3]
            col = meta[src, c * 3 + 1]
            weight = (at < n_live).astype(f32)
            picks.append((src, c, row, col, weight, lane >= col))

        def window(b, s, r):
            _, _, row, _, _, mask = picks[b]
            return tuple(
                jnp.where(
                    mask,
                    slab[part * 2 + s, 0, pl.ds(row + r, CHUNK), :],
                    slab[part * 2 + s, 1, pl.ds(row + r, CHUNK), :],
                )
                for part in range(2)
            )

        def add_term(b, s, r, term):
            _, _, row, _, _, mask = picks[b]
            for part in range(2):
                for h in range(2):
                    spot = acc.at[part * 2 + s, h, pl.ds(row + r, CHUNK), :]
                    pltpu.store(spot, spot[...] + term[part], mask=mask if h == 0 else ~mask)

        def enter(group):
            for b in members(group):
                shift = lax.rem(picks[b][3], edge)
                for r in chunks:
                    at = b * edge + r
                    re = pltpu.roll(probe[0, r : r + CHUNK, :], shift, 1)
                    im = pltpu.roll(probe[1, r : r + CHUNK, :], shift, 1)
                    rolled[at : at + CHUNK, :edge] = re
                    rolled[at : at + CHUNK, edge:] = im
                    keep(b, r, times((re, im), window(b, 0, r)))

        def leave(group):
            for b in members(group):
                for r in chunks:
                    at = b * edge + r
                    slab_part = window(b, 1, r)
                    cut[at : at + CHUNK, :edge] = slab_part[0]
                    cut[at : at + CHUNK, edge:] = slab_part[1]
                    keep(b, r, times(read(wave, b, r), slab_part))

        def compare(group):
            for b in members(group):
                src, c, _, _, weight, _ = picks[b]
                for r in chunks:
                    re, im = read(field, b, r)
                    start = pl.multiple_of(c * edge + r, CHUNK)
                    measured = payload[src, pl.ds(start, CHUNK), :].astype(f32)
                    excess = weight * (re * re + im * im - measured)
                    keep(b, r, (excess * re, excess * im))

        def turn(group):
            for b in members(group):
                for r in chunks:
                    back = read(field, b, r)
                    add_term(b, 1, r, conj_times(read(wave, b, r), back))
                    keep(b, r, conj_times(read(cut, b, r), back))

        def close(group):
            for b in members(group):
                for r in chunks:
                    add_term(b, 0, r, conj_times(read(rolled, b, r), read(field, b, r)))

        steps = (
            enter,
            lambda g: apply_left(g, 0),
            lambda g: apply_right(g, 1, wave),
            leave,
            lambda g: apply_left(g, 2),
            lambda g: apply_right(g, 3, field),
            compare,
            lambda g: apply_left(g, 3),
            lambda g: apply_right(g, 2, field),
            turn,
            lambda g: apply_left(g, 1),
            lambda g: apply_right(g, 0, field),
            close,
        )
        n_groups = BATCH // GROUP
        for t in range(len(steps) + (n_groups - 1) * SKEW):
            for g in range(n_groups):
                if 0 <= t - g * SKEW < len(steps):
                    steps[t - g * SKEW](g)
        return carry

    lax.fori_loop(0, (n_live + BATCH - 1) // BATCH, run_batch, 0)

    def emit(p, carry):
        at = pl.multiple_of(p * strip, 8)
        for a in range(4):
            for h, ref in enumerate((own_out, spill_out)):
                ref[p, a * strip : (a + 1) * strip, :] = acc[a, h, pl.ds(at, strip), :].astype(bf16)
        return carry

    lax.fori_loop(0, own_out.shape[0], emit, 0, unroll=4)


def local_gradient(here, meta, payload, strips, tables, probe, cap):
    edge = probe.shape[1]
    n_pos = 2 * strips[0].shape[0]
    rows = n_pos * strips[0].shape[1] // 4
    share = jax.ShapeDtypeStruct((n_pos, *strips[0].shape[1:]), jnp.bfloat16)
    smem = pl.BlockSpec(memory_space=pltpu.SMEM)
    vmem = pl.BlockSpec(memory_space=pltpu.VMEM)
    return pl.pallas_call(
        functools.partial(grad_kernel, cap=cap),
        out_shape=(share, share),
        in_specs=[smem, smem, vmem, vmem, vmem, vmem, vmem, vmem, vmem],
        out_specs=(vmem, vmem),
        scratch_shapes=[
            pltpu.VMEM((4, 2, rows, edge), jnp.float32),
            pltpu.VMEM((4, 2, rows, edge), jnp.float32),
            pltpu.SMEM((meta.shape[0] * cap + BATCH,), jnp.int32),
            pltpu.VMEM((2 * edge, BATCH * edge), jnp.bfloat16),
            pltpu.VMEM((BATCH * edge, 2 * edge), jnp.bfloat16),
            pltpu.VMEM((BATCH * edge, 2 * edge), jnp.float32),
            pltpu.VMEM((BATCH * edge, 2 * edge), jnp.float32),
            pltpu.VMEM((BATCH * edge, 2 * edge), jnp.float32),
            pltpu.VMEM((BATCH * edge, 2 * edge), jnp.float32),
        ],
        compiler_params=pltpu.CompilerParams(vmem_limit_bytes=48 * 1024 * 1024),
        name="local_gradient",
    )(here, meta, payload, *strips, tables, probe)


def moved(value, tile_step, flip):
    n_tile, n_pos = lax.axis_size("tile"), lax.axis_size("pos")
    pairs = []
    for t in range(n_tile):
        if 0 <= t + tile_step < n_tile:
            for p in range(n_pos):
                source = (t + tile_step) * n_pos + (p ^ 1 if flip else p)
                pairs.append((source, t * n_pos + p))
    return lax.ppermute(value, ("tile", "pos"), pairs)


def body(
    patterns, coords, send_slots, send_counts, object_real, object_imag, probe_real, probe_imag
):
    edge_len = probe_real.shape[0]
    slices, strip, tile_width = object_real.shape
    n_pos = lax.axis_size("pos")
    per_source = patterns.shape[0]
    cap = send_slots.shape[2]

    sent = spread(object_real, object_imag, n_pos // 2)
    same_y = [[2 * z + y for z in range(n_pos // 2)] for y in range(2)]
    mine = lax.all_to_all(sent, "pos", 0, 0, axis_index_groups=same_y, tiled=True)

    payload = pack(
        patterns,
        coords.T,
        send_slots[0].T,
        send_counts,
        cap,
        tile_width,
        n_pos * strip - edge_len,
    )
    mine, payload = lax.optimization_barrier((mine, payload))
    other = moved(mine, 0, True)
    other_next = moved(mine, 1, True)
    strips = (mine, other, other_next, moved(mine, 1, False))
    payload = lax.all_to_all(payload, "tile", 0, 0, tiled=True)
    meta = payload[:, cap * edge_len, :].astype(jnp.int32)

    own, spill = local_gradient(
        (lax.axis_index("pos") % 2).astype(jnp.int32).reshape(1),
        meta,
        payload,
        strips,
        jnp.asarray(host_tables(edge_len)),
        jnp.stack([probe_real, probe_imag]),
        cap,
    )
    total = own.astype(jnp.float32) + moved(spill, -1, False).astype(jnp.float32)
    pieces = lax.all_to_all(total.astype(jnp.bfloat16), "pos", 0, 0, tiled=True)
    share = jnp.sum(pieces.astype(jnp.float32), axis=0)
    share = share * (1.0 / math.sqrt(per_source * n_pos))
    share = share.reshape(2, slices, strip, tile_width)
    return (share[0], share[1])


def solution(mesh):
    in_specs = (
        P(("tile", "pos"), None, None),
        P(("tile", "pos"), None),
        P(("tile", "pos"), None, None),
        P(("tile", "pos"), None),
        P(None, "pos", "tile"),
        P(None, "pos", "tile"),
        P(),
        P(),
    )
    out_specs = (P(None, "pos", "tile"), P(None, "pos", "tile"))
    return jax.shard_map(body, mesh=mesh, in_specs=in_specs, out_specs=out_specs, check_vma=False)
```

```python
import functools
import math

import jax
import jax.numpy as jnp
import ml_dtypes
import numpy as np
from jax import lax
from jax.experimental import pallas as pl
from jax.experimental.pallas import tpu as pltpu
from jax.sharding import PartitionSpec as P

BATCH = 16
GROUP = 8
SKEW = 1
CHUNK = 16
META_ROWS = 16


def host_tables(edge_len):
    indices = np.arange(edge_len)
    phases = (indices[:, None] * indices[None, :] % edge_len) * (2.0 * math.pi / edge_len)
    wave = np.exp(1j * phases) / math.sqrt(edge_len)
    centred = np.where(indices < edge_len // 2, indices, indices - edge_len)
    kern = np.exp(-0.5j * math.pi * centred * centred / edge_len)
    fresnel = (wave * kern[None, :]) @ wave.conj().T
    fresnel = 0.5 * (fresnel + fresnel.T)

    def rounded(x):
        return x.astype(np.float32).astype(ml_dtypes.bfloat16)

    def left(re, im):
        return np.block([[re, -im], [im, re]])

    def right(re, im):
        return np.block([[re, im], [-im, re]])

    fr, fi = rounded(fresnel.real), rounded(fresnel.imag)
    dr, di = rounded(wave.real), rounded(-wave.imag)
    return np.stack([left(fr, fi), right(fr, fi), left(dr, di), right(dr, di)])


def spread_kernel(real, imag, out):
    parts = [ref[s] for ref in (real, imag) for s in range(real.shape[0])]
    joined = jnp.concatenate(parts, axis=0).astype(jnp.bfloat16)
    for z in range(out.shape[0]):
        out[z] = joined


def spread(real, imag, copies):
    vmem = pl.BlockSpec(memory_space=pltpu.VMEM)
    slices, strip, width = real.shape
    return pl.pallas_call(
        spread_kernel,
        out_shape=jax.ShapeDtypeStruct((copies, 2 * slices * strip, width), jnp.bfloat16),
        in_specs=[vmem, vmem],
        out_specs=vmem,
        name="spread",
    )(real, imag)


def pack_kernel(slots, counts, coords, patterns, out, *, n_tile, cap, tile_width, row_max):
    rows = patterns.shape[1]
    lane = lax.broadcasted_iota(jnp.int32, (META_ROWS, 128), 1)
    for d in range(n_tile):
        value = jnp.zeros((META_ROWS, 128), jnp.int32)
        for c in range(cap):
            j = slots[c, d]
            out[d, c * rows : (c + 1) * rows, :] = patterns[j]
            row = jnp.clip(coords[0, j], 0, row_max)
            col = jnp.clip(coords[1, j] - d * tile_width, 0, tile_width)
            live = (c < counts[0, d]).astype(jnp.int32)
            for k, part in enumerate((row, col, live)):
                value = jnp.where(lane == 3 * c + k, part, value)
        out[d, cap * rows :, :] = value.astype(jnp.float32).astype(jnp.bfloat16)


def pack(patterns, coords, send_slots, send_counts, cap, tile_width, row_max):
    rows = patterns.shape[1]
    n_tile = send_counts.shape[1]
    body = functools.partial(
        pack_kernel, n_tile=n_tile, cap=cap, tile_width=tile_width, row_max=row_max
    )
    smem = pl.BlockSpec(memory_space=pltpu.SMEM)
    vmem = pl.BlockSpec(memory_space=pltpu.VMEM)
    return pl.pallas_call(
        body,
        out_shape=jax.ShapeDtypeStruct((n_tile, cap * rows + META_ROWS, 128), jnp.bfloat16),
        in_specs=[smem, smem, smem, vmem],
        out_specs=vmem,
        name="pack",
    )(send_slots, send_counts, coords, patterns)


def grad_kernel(
    here,
    meta,
    payload,
    mine,
    other,
    other_next,
    mine_next,
    tables,
    probe,
    own_kept,
    own_given,
    spill_kept,
    spill_given,
    slab,
    acc,
    order,
    data,
    half,
    field,
    wave,
    rolled,
    cut,
    *,
    cap,
):
    edge = probe.shape[1]
    bf16, f32 = jnp.bfloat16, jnp.float32
    strip = mine.shape[1] // 4
    slot_count = meta.shape[0] * cap

    for i in range(slot_count + BATCH):
        order[i] = 0

    n_live = jnp.int32(0)
    for i in range(slot_count):
        order[n_live] = i
        n_live += meta[i // cap, (i % cap) * 3 + 2]

    def unpack(z, carry):
        for ref, y, h in (
            (mine, here[0], 0),
            (mine_next, here[0], 1),
            (other, 1 - here[0], 0),
            (other_next, 1 - here[0], 1),
        ):
            block = ref[z].astype(f32)
            at = pl.multiple_of((2 * z + y) * strip, 8)
            for a in range(4):
                slab[a, h, pl.ds(at, strip), :] = block[a * strip : (a + 1) * strip]
        return carry

    lax.fori_loop(0, mine.shape[0], unpack, 0, unroll=4)
    acc[...] = jnp.zeros(acc.shape, f32)

    lane = lax.broadcasted_iota(jnp.int32, (CHUNK, edge), 1)
    dot = functools.partial(jnp.dot, preferred_element_type=f32)
    chunks = range(0, edge, CHUNK)

    def apply_left(group, left):
        for b in range(group * GROUP, (group + 1) * GROUP, 2):
            full = dot(tables[left], data[:, b * edge : (b + 2) * edge]).astype(bf16)
            for h in range(2):
                for k in range(2):
                    half[(b + h) * edge : (b + h + 1) * edge, k * edge : (k + 1) * edge] = full[
                        k * edge : (k + 1) * edge, h * edge : (h + 1) * edge
                    ]

    def apply_right(group, right, target):
        at = group * GROUP * edge
        target[at : at + GROUP * edge, :] = dot(half[at : at + GROUP * edge, :], tables[right])

    def times(a, b):
        return (a[0] * b[0] - a[1] * b[1], a[0] * b[1] + a[1] * b[0])

    def conj_times(a, b):
        return (a[0] * b[0] + a[1] * b[1], a[0] * b[1] - a[1] * b[0])

    def keep(b, r, z):
        for k in range(2):
            data[k * edge + r : k * edge + r + CHUNK, b * edge : (b + 1) * edge] = z[k].astype(bf16)

    def read(ref, b, r):
        at = b * edge + r
        return (ref[at : at + CHUNK, :edge], ref[at : at + CHUNK, edge:])

    def members(group):
        return range(group * GROUP, (group + 1) * GROUP)

    def run_batch(i, carry):
        picks = []
        for b in range(BATCH):
            at = i * BATCH + b
            s = order[at]
            src, c = s // cap, s % cap
            row = meta[src, c * 3]
            col = meta[src, c * 3 + 1]
            weight = (at < n_live).astype(f32)
            picks.append((src, c, row, col, weight, lane >= col))

        def window(b, s, r):
            _, _, row, _, _, mask = picks[b]
            return tuple(
                jnp.where(
                    mask,
                    slab[part * 2 + s, 0, pl.ds(row + r, CHUNK), :],
                    slab[part * 2 + s, 1, pl.ds(row + r, CHUNK), :],
                )
                for part in range(2)
            )

        def add_term(b, s, r, term):
            _, _, row, _, _, mask = picks[b]
            for part in range(2):
                for h in range(2):
                    spot = acc.at[part * 2 + s, h, pl.ds(row + r, CHUNK), :]
                    pltpu.store(spot, spot[...] + term[part], mask=mask if h == 0 else ~mask)

        def enter(group):
            for b in members(group):
                shift = lax.rem(picks[b][3], edge)
                for r in chunks:
                    at = b * edge + r
                    re = pltpu.roll(probe[0, r : r + CHUNK, :], shift, 1)
                    im = pltpu.roll(probe[1, r : r + CHUNK, :], shift, 1)
                    rolled[at : at + CHUNK, :edge] = re
                    rolled[at : at + CHUNK, edge:] = im
                    keep(b, r, times((re, im), window(b, 0, r)))

        def leave(group):
            for b in members(group):
                for r in chunks:
                    at = b * edge + r
                    slab_part = window(b, 1, r)
                    cut[at : at + CHUNK, :edge] = slab_part[0]
                    cut[at : at + CHUNK, edge:] = slab_part[1]
                    keep(b, r, times(read(wave, b, r), slab_part))

        def compare(group):
            for b in members(group):
                src, c, _, _, weight, _ = picks[b]
                for r in chunks:
                    re, im = read(field, b, r)
                    start = pl.multiple_of(c * edge + r, CHUNK)
                    measured = payload[src, pl.ds(start, CHUNK), :].astype(f32)
                    excess = weight * (re * re + im * im - measured)
                    keep(b, r, (excess * re, excess * im))

        def turn(group):
            for b in members(group):
                for r in chunks:
                    back = read(field, b, r)
                    add_term(b, 1, r, conj_times(read(wave, b, r), back))
                    keep(b, r, conj_times(read(cut, b, r), back))

        def close(group):
            for b in members(group):
                for r in chunks:
                    add_term(b, 0, r, conj_times(read(rolled, b, r), read(field, b, r)))

        steps = (
            enter,
            lambda g: apply_left(g, 0),
            lambda g: apply_right(g, 1, wave),
            leave,
            lambda g: apply_left(g, 2),
            lambda g: apply_right(g, 3, field),
            compare,
            lambda g: apply_left(g, 3),
            lambda g: apply_right(g, 2, field),
            turn,
            lambda g: apply_left(g, 1),
            lambda g: apply_right(g, 0, field),
            close,
        )
        n_groups = BATCH // GROUP
        for t in range(len(steps) + (n_groups - 1) * SKEW):
            for g in range(n_groups):
                if 0 <= t - g * SKEW < len(steps):
                    steps[t - g * SKEW](g)
        return carry

    lax.fori_loop(0, (n_live + BATCH - 1) // BATCH, run_batch, 0)

    def emit(z, carry):
        for ref, y, h in (
            (own_kept, here[0], 0),
            (own_given, 1 - here[0], 0),
            (spill_kept, here[0], 1),
            (spill_given, 1 - here[0], 1),
        ):
            at = pl.multiple_of((2 * z + y) * strip, 8)
            for a in range(4):
                ref[z, a * strip : (a + 1) * strip, :] = acc[a, h, pl.ds(at, strip), :].astype(bf16)
        return carry

    lax.fori_loop(0, own_kept.shape[0], emit, 0, unroll=4)


def local_gradient(here, meta, payload, strips, tables, probe, cap):
    edge = probe.shape[1]
    n_pos = 2 * strips[0].shape[0]
    rows = n_pos * strips[0].shape[1] // 4
    share = jax.ShapeDtypeStruct(strips[0].shape, jnp.bfloat16)
    smem = pl.BlockSpec(memory_space=pltpu.SMEM)
    vmem = pl.BlockSpec(memory_space=pltpu.VMEM)
    return pl.pallas_call(
        functools.partial(grad_kernel, cap=cap),
        out_shape=(share,) * 4,
        in_specs=[smem, smem, vmem, vmem, vmem, vmem, vmem, vmem, vmem],
        out_specs=(vmem,) * 4,
        scratch_shapes=[
            pltpu.VMEM((4, 2, rows, edge), jnp.float32),
            pltpu.VMEM((4, 2, rows, edge), jnp.float32),
            pltpu.SMEM((meta.shape[0] * cap + BATCH,), jnp.int32),
            pltpu.VMEM((2 * edge, BATCH * edge), jnp.bfloat16),
            pltpu.VMEM((BATCH * edge, 2 * edge), jnp.bfloat16),
            pltpu.VMEM((BATCH * edge, 2 * edge), jnp.float32),
            pltpu.VMEM((BATCH * edge, 2 * edge), jnp.float32),
            pltpu.VMEM((BATCH * edge, 2 * edge), jnp.float32),
            pltpu.VMEM((BATCH * edge, 2 * edge), jnp.float32),
        ],
        compiler_params=pltpu.CompilerParams(vmem_limit_bytes=48 * 1024 * 1024),
        name="local_gradient",
    )(here, meta, payload, *strips, tables, probe)


def moved(value, tile_step, flip):
    n_tile, n_pos = lax.axis_size("tile"), lax.axis_size("pos")
    pairs = []
    for t in range(n_tile):
        if 0 <= t + tile_step < n_tile:
            for p in range(n_pos):
                source = (t + tile_step) * n_pos + (p ^ 1 if flip else p)
                pairs.append((source, t * n_pos + p))
    return lax.ppermute(value, ("tile", "pos"), pairs)


def body(
    patterns, coords, send_slots, send_counts, object_real, object_imag, probe_real, probe_imag
):
    edge_len = probe_real.shape[0]
    slices, strip, tile_width = object_real.shape
    n_pos = lax.axis_size("pos")
    per_source = patterns.shape[0]
    cap = send_slots.shape[2]

    sent = spread(object_real, object_imag, n_pos // 2)
    same_y = [[2 * z + y for z in range(n_pos // 2)] for y in range(2)]
    mine = lax.all_to_all(sent, "pos", 0, 0, axis_index_groups=same_y, tiled=True)

    payload = pack(
        patterns,
        coords.T,
        send_slots[0].T,
        send_counts,
        cap,
        tile_width,
        n_pos * strip - edge_len,
    )
    mine, payload = lax.optimization_barrier((mine, payload))
    other = moved(mine, 0, True)
    other_next = moved(mine, 1, True)
    strips = (mine, other, other_next, moved(mine, 1, False))
    payload = lax.all_to_all(payload, "tile", 0, 0, tiled=True)
    meta = payload[:, cap * edge_len, :].astype(jnp.int32)

    own_kept, own_given, spill_kept, spill_given = local_gradient(
        (lax.axis_index("pos") % 2).astype(jnp.int32).reshape(1),
        meta,
        payload,
        strips,
        jnp.asarray(host_tables(edge_len)),
        jnp.stack([probe_real, probe_imag]),
        cap,
    )
    total = own_kept.astype(jnp.float32)
    total += moved(own_given, 0, True).astype(jnp.float32)
    total += moved(spill_given, -1, True).astype(jnp.float32)
    total += moved(spill_kept, -1, False).astype(jnp.float32)
    pieces = lax.all_to_all(
        total.astype(jnp.bfloat16), "pos", 0, 0, axis_index_groups=same_y, tiled=True
    )
    share = jnp.sum(pieces.astype(jnp.float32), axis=0)
    share = share * (1.0 / math.sqrt(per_source * n_pos))
    share = share.reshape(2, slices, strip, tile_width)
    return (share[0], share[1])


def solution(mesh):
    in_specs = (
        P(("tile", "pos"), None, None),
        P(("tile", "pos"), None),
        P(("tile", "pos"), None, None),
        P(("tile", "pos"), None),
        P(None, "pos", "tile"),
        P(None, "pos", "tile"),
        P(),
        P(),
    )
    out_specs = (P(None, "pos", "tile"), P(None, "pos", "tile"))
    return jax.shard_map(body, mesh=mesh, in_specs=in_specs, out_specs=out_specs, check_vma=False)
```

```python
import functools
import math

import jax
import jax.numpy as jnp
import ml_dtypes
import numpy as np
from jax import lax
from jax.experimental import pallas as pl
from jax.experimental.pallas import tpu as pltpu
from jax.sharding import PartitionSpec as P

BATCH = 16
GROUP = 8
SKEW = 1
CHUNK = 16
META_ROWS = 16


def host_tables(edge_len):
    indices = np.arange(edge_len)
    phases = (indices[:, None] * indices[None, :] % edge_len) * (2.0 * math.pi / edge_len)
    wave = np.exp(1j * phases) / math.sqrt(edge_len)
    centred = np.where(indices < edge_len // 2, indices, indices - edge_len)
    kern = np.exp(-0.5j * math.pi * centred * centred / edge_len)
    fresnel = (wave * kern[None, :]) @ wave.conj().T
    fresnel = 0.5 * (fresnel + fresnel.T)

    def rounded(x):
        return x.astype(np.float32).astype(ml_dtypes.bfloat16)

    def left(re, im):
        return np.block([[re, -im], [im, re]])

    def right(re, im):
        return np.block([[re, im], [-im, re]])

    fr, fi = rounded(fresnel.real), rounded(fresnel.imag)
    dr, di = rounded(wave.real), rounded(-wave.imag)
    return np.stack([left(fr, fi), right(fr, fi), left(dr, di), right(dr, di)])


def spread_kernel(real, imag, out):
    parts = [ref[s] for ref in (real, imag) for s in range(real.shape[0])]
    joined = jnp.concatenate(parts, axis=0).astype(jnp.bfloat16)
    for z in range(out.shape[0]):
        out[z] = joined


def spread(real, imag, copies):
    vmem = pl.BlockSpec(memory_space=pltpu.VMEM)
    slices, strip, width = real.shape
    return pl.pallas_call(
        spread_kernel,
        out_shape=jax.ShapeDtypeStruct((copies, 2 * slices * strip, width), jnp.bfloat16),
        in_specs=[vmem, vmem],
        out_specs=vmem,
        name="spread",
    )(real, imag)


def pack_kernel(slots, counts, coords, patterns, out, *, n_tile, cap, tile_width, row_max):
    rows = patterns.shape[1]
    lane = lax.broadcasted_iota(jnp.int32, (META_ROWS, 128), 1)
    for d in range(n_tile):
        value = jnp.zeros((META_ROWS, 128), jnp.int32)
        for c in range(cap):
            j = slots[c, d]
            out[d, c * rows : (c + 1) * rows, :] = patterns[j]
            row = jnp.clip(coords[0, j], 0, row_max)
            col = jnp.clip(coords[1, j] - d * tile_width, 0, tile_width)
            live = (c < counts[0, d]).astype(jnp.int32)
            for k, part in enumerate((row, col, live)):
                value = jnp.where(lane == 3 * c + k, part, value)
        out[d, cap * rows :, :] = value.astype(jnp.float32).astype(jnp.bfloat16)


def pack(patterns, coords, send_slots, send_counts, cap, tile_width, row_max):
    rows = patterns.shape[1]
    n_tile = send_counts.shape[1]
    body = functools.partial(
        pack_kernel, n_tile=n_tile, cap=cap, tile_width=tile_width, row_max=row_max
    )
    smem = pl.BlockSpec(memory_space=pltpu.SMEM)
    vmem = pl.BlockSpec(memory_space=pltpu.VMEM)
    return pl.pallas_call(
        body,
        out_shape=jax.ShapeDtypeStruct((n_tile, cap * rows + META_ROWS, 128), jnp.bfloat16),
        in_specs=[smem, smem, smem, vmem],
        out_specs=vmem,
        name="pack",
    )(send_slots, send_counts, coords, patterns)


def grad_kernel(
    here,
    meta,
    payload,
    mine,
    other,
    other_next,
    mine_next,
    tables,
    probe,
    own_kept,
    own_given,
    spill_kept,
    spill_given,
    slab,
    acc,
    order,
    data,
    half,
    field,
    wave,
    rolled,
    cut,
    *,
    cap,
):
    edge = probe.shape[1]
    bf16, f32 = jnp.bfloat16, jnp.float32
    strip = mine.shape[1] // 4
    slot_count = meta.shape[0] * cap

    for i in range(slot_count + BATCH):
        order[i] = 0

    n_live = jnp.int32(0)
    for i in range(slot_count):
        order[n_live] = i
        n_live += meta[i // cap, (i % cap) * 3 + 2]

    def unpack(z, carry):
        for ref, y, h in (
            (mine, here[0], 0),
            (mine_next, here[0], 1),
            (other, 1 - here[0], 0),
            (other_next, 1 - here[0], 1),
        ):
            block = ref[z].astype(f32)
            at = pl.multiple_of((2 * z + y) * strip, 8)
            for a in range(4):
                slab[a, h, pl.ds(at, strip), :] = block[a * strip : (a + 1) * strip]
        return carry

    lax.fori_loop(0, mine.shape[0], unpack, 0, unroll=4)
    acc[...] = jnp.zeros(acc.shape, f32)

    lane = lax.broadcasted_iota(jnp.int32, (CHUNK, edge), 1)
    dot = functools.partial(jnp.dot, preferred_element_type=f32)
    chunks = range(0, edge, CHUNK)

    def apply_left(group, left):
        for b in range(group * GROUP, (group + 1) * GROUP, 2):
            full = dot(tables[left], data[:, b * edge : (b + 2) * edge]).astype(bf16)
            for h in range(2):
                for k in range(2):
                    half[(b + h) * edge : (b + h + 1) * edge, k * edge : (k + 1) * edge] = full[
                        k * edge : (k + 1) * edge, h * edge : (h + 1) * edge
                    ]

    def apply_right(group, right, target):
        at = group * GROUP * edge
        target[at : at + GROUP * edge, :] = dot(half[at : at + GROUP * edge, :], tables[right])

    def times(a, b):
        return (a[0] * b[0] - a[1] * b[1], a[0] * b[1] + a[1] * b[0])

    def conj_times(a, b):
        return (a[0] * b[0] + a[1] * b[1], a[0] * b[1] - a[1] * b[0])

    def keep(b, r, z):
        for k in range(2):
            data[k * edge + r : k * edge + r + CHUNK, b * edge : (b + 1) * edge] = z[k].astype(bf16)

    def read(ref, b, r):
        at = b * edge + r
        return (ref[at : at + CHUNK, :edge], ref[at : at + CHUNK, edge:])

    def members(group):
        return range(group * GROUP, (group + 1) * GROUP)

    def run_batch(i, carry):
        picks = []
        for b in range(BATCH):
            at = i * BATCH + b
            s = order[at]
            src, c = s // cap, s % cap
            row = meta[src, c * 3]
            col = meta[src, c * 3 + 1]
            weight = (at < n_live).astype(f32)
            picks.append((src, c, row, col, weight, lane >= col))

        def window(b, s, r):
            _, _, row, _, _, mask = picks[b]
            return tuple(
                jnp.where(
                    mask,
                    slab[part * 2 + s, 0, pl.ds(row + r, CHUNK), :],
                    slab[part * 2 + s, 1, pl.ds(row + r, CHUNK), :],
                )
                for part in range(2)
            )

        def add_term(b, s, r, term):
            _, _, row, _, _, mask = picks[b]
            for part in range(2):
                for h in range(2):
                    spot = acc.at[part * 2 + s, h, pl.ds(row + r, CHUNK), :]
                    pltpu.store(spot, spot[...] + term[part], mask=mask if h == 0 else ~mask)

        def enter(group):
            for b in members(group):
                shift = lax.rem(picks[b][3], edge)
                for r in chunks:
                    at = b * edge + r
                    re = pltpu.roll(probe[0, r : r + CHUNK, :], shift, 1)
                    im = pltpu.roll(probe[1, r : r + CHUNK, :], shift, 1)
                    rolled[at : at + CHUNK, :edge] = re
                    rolled[at : at + CHUNK, edge:] = im
                    keep(b, r, times((re, im), window(b, 0, r)))

        def leave(group):
            for b in members(group):
                for r in chunks:
                    at = b * edge + r
                    slab_part = window(b, 1, r)
                    cut[at : at + CHUNK, :edge] = slab_part[0]
                    cut[at : at + CHUNK, edge:] = slab_part[1]
                    keep(b, r, times(read(wave, b, r), slab_part))

        def compare(group):
            for b in members(group):
                src, c, _, _, weight, _ = picks[b]
                for r in chunks:
                    re, im = read(field, b, r)
                    start = pl.multiple_of(c * edge + r, CHUNK)
                    measured = payload[src, pl.ds(start, CHUNK), :].astype(f32)
                    excess = weight * (re * re + im * im - measured)
                    keep(b, r, (excess * re, excess * im))

        def turn(group):
            for b in members(group):
                for r in chunks:
                    back = read(field, b, r)
                    add_term(b, 1, r, conj_times(read(wave, b, r), back))
                    keep(b, r, conj_times(read(cut, b, r), back))

        def close(group):
            for b in members(group):
                for r in chunks:
                    add_term(b, 0, r, conj_times(read(rolled, b, r), read(field, b, r)))

        steps = (
            enter,
            lambda g: apply_left(g, 0),
            lambda g: apply_right(g, 1, wave),
            leave,
            lambda g: apply_left(g, 2),
            lambda g: apply_right(g, 3, field),
            compare,
            lambda g: apply_left(g, 3),
            lambda g: apply_right(g, 2, field),
            turn,
            lambda g: apply_left(g, 1),
            lambda g: apply_right(g, 0, field),
            close,
        )
        n_groups = BATCH // GROUP
        for t in range(len(steps) + (n_groups - 1) * SKEW):
            for g in range(n_groups):
                if 0 <= t - g * SKEW < len(steps):
                    steps[t - g * SKEW](g)
        return carry

    lax.fori_loop(0, (n_live + BATCH - 1) // BATCH, run_batch, 0)

    def emit(z, carry):
        for ref, y, h in (
            (own_kept, here[0], 0),
            (own_given, 1 - here[0], 0),
            (spill_kept, here[0], 1),
            (spill_given, 1 - here[0], 1),
        ):
            at = pl.multiple_of((2 * z + y) * strip, 8)
            for a in range(4):
                ref[z, a * strip : (a + 1) * strip, :] = acc[a, h, pl.ds(at, strip), :].astype(bf16)
        return carry

    lax.fori_loop(0, own_kept.shape[0], emit, 0, unroll=4)


def local_gradient(here, meta, payload, strips, tables, probe, cap):
    edge = probe.shape[1]
    n_pos = 2 * strips[0].shape[0]
    rows = n_pos * strips[0].shape[1] // 4
    share = jax.ShapeDtypeStruct(strips[0].shape, jnp.bfloat16)
    smem = pl.BlockSpec(memory_space=pltpu.SMEM)
    vmem = pl.BlockSpec(memory_space=pltpu.VMEM)
    return pl.pallas_call(
        functools.partial(grad_kernel, cap=cap),
        out_shape=(share,) * 4,
        in_specs=[smem, smem, vmem, vmem, vmem, vmem, vmem, vmem, vmem],
        out_specs=(vmem,) * 4,
        scratch_shapes=[
            pltpu.VMEM((4, 2, rows, edge), jnp.float32),
            pltpu.VMEM((4, 2, rows, edge), jnp.float32),
            pltpu.SMEM((meta.shape[0] * cap + BATCH,), jnp.int32),
            pltpu.VMEM((2 * edge, BATCH * edge), jnp.bfloat16),
            pltpu.VMEM((BATCH * edge, 2 * edge), jnp.bfloat16),
            pltpu.VMEM((BATCH * edge, 2 * edge), jnp.float32),
            pltpu.VMEM((BATCH * edge, 2 * edge), jnp.float32),
            pltpu.VMEM((BATCH * edge, 2 * edge), jnp.float32),
            pltpu.VMEM((BATCH * edge, 2 * edge), jnp.float32),
        ],
        compiler_params=pltpu.CompilerParams(vmem_limit_bytes=48 * 1024 * 1024),
        name="local_gradient",
    )(here, meta, payload, *strips, tables, probe)


def moved(value, tile_step, flip):
    n_tile, n_pos = lax.axis_size("tile"), lax.axis_size("pos")
    pairs = []
    for t in range(n_tile):
        if 0 <= t + tile_step < n_tile:
            for p in range(n_pos):
                source = (t + tile_step) * n_pos + (p ^ 1 if flip else p)
                pairs.append((source, t * n_pos + p))
    return lax.ppermute(value, ("tile", "pos"), pairs)


def body(
    patterns, coords, send_slots, send_counts, object_real, object_imag, probe_real, probe_imag
):
    edge_len = probe_real.shape[0]
    slices, strip, tile_width = object_real.shape
    n_pos = lax.axis_size("pos")
    per_source = patterns.shape[0]
    cap = send_slots.shape[2]

    sent = spread(object_real, object_imag, n_pos // 2)
    same_y = [[2 * z + y for z in range(n_pos // 2)] for y in range(2)]
    mine = lax.all_to_all(sent, "pos", 0, 0, axis_index_groups=same_y, tiled=True)

    payload = pack(
        patterns,
        coords.T,
        send_slots[0].T,
        send_counts,
        cap,
        tile_width,
        n_pos * strip - edge_len,
    )
    mine, payload = lax.optimization_barrier((mine, payload))
    other = moved(mine, 0, True)
    other_next = moved(mine, 1, True)
    strips = (mine, other, other_next, moved(mine, 1, False))
    payload = lax.all_to_all(payload, "tile", 0, 0, tiled=True)
    meta = payload[:, cap * edge_len, :].astype(jnp.int32)

    own_kept, own_given, spill_kept, spill_given = local_gradient(
        (lax.axis_index("pos") % 2).astype(jnp.int32).reshape(1),
        meta,
        payload,
        strips,
        jnp.asarray(host_tables(edge_len)),
        jnp.stack([probe_real, probe_imag]),
        cap,
    )
    total = own_kept.astype(jnp.float32)
    total += moved(spill_kept, -1, False).astype(jnp.float32)
    total += moved(spill_given, -1, True).astype(jnp.float32)
    total += moved(own_given, 0, True).astype(jnp.float32)
    pieces = lax.all_to_all(
        total.astype(jnp.bfloat16), "pos", 0, 0, axis_index_groups=same_y, tiled=True
    )
    share = jnp.sum(pieces.astype(jnp.float32), axis=0)
    share = share * (1.0 / math.sqrt(per_source * n_pos))
    share = share.reshape(2, slices, strip, tile_width)
    return (share[0], share[1])


def solution(mesh):
    in_specs = (
        P(("tile", "pos"), None, None),
        P(("tile", "pos"), None),
        P(("tile", "pos"), None, None),
        P(("tile", "pos"), None),
        P(None, "pos", "tile"),
        P(None, "pos", "tile"),
        P(),
        P(),
    )
    out_specs = (P(None, "pos", "tile"), P(None, "pos", "tile"))
    return jax.shard_map(body, mesh=mesh, in_specs=in_specs, out_specs=out_specs, check_vma=False)
```
